32 devices in a mesh: ulysses: 4 (over z), blk: 2 (over y), tensor: 4 (over x, core).
Axes of the slice: x: 2, y: 2, z: 4, core: 2. Of those that a mesh axis runs over, the one named last changes fastest.
Arguments:
- tokens: bfloat16 [2048, 5120], P(('ulysses', 'blk'), 'tensor'), may hold values from -20 to 20
- w_qkv: bfloat16 [5120, 3, 4096], P(None, None, ('ulysses', 'tensor')), may hold values from -2 to 2
- qkv_scale: float32 [3, 32], P(None, ('ulysses', 'tensor')), may hold values from 0.6 to 9
- block_mask: int32 [32, 16, 16], P(('ulysses', 'tensor')), may hold values from 0 to 1, as said below
- w_out: bfloat16 [4, 1024, 5120], P(None, 'tensor'), may hold values from -0.125 to 0.125
Outputs:
- mixed: bfloat16 [2048, 5120], P(('ulysses', 'blk'), 'tensor')
The draws below stay inside these ranges and needn't reach their ends.
Inputs may be any that keep to these rules, and one draw needn't show every extreme that they name: `block_mask`: 0 or 1; the share of ones differs from head to head.
All inputs are finite; a program needn't handle non-finite values.
Results may differ from the reference program's by a relative error of at most 0.015.
Values may be sent and summed in bfloat16 or wider, within the bound.
A program may use at most 128 MiB of HBM per device.

```python
import math
import jax
import jax.numpy as jnp
from jax import lax

D = 5120
HD = 128
HPD = 2
BLOCK = 128
HEADS = 32
TOKENS = 2048
NB = 16
N_ULYSSES = 4
N_TENSOR = 4


def draw_block_mask(key, part):
    dense_key = jax.random.fold_in(key, 11)
    cell_key = jax.random.fold_in(key, 12)
    density = jax.random.randint(dense_key, (HEADS, 1, 1), 1, 8)
    cells = jax.random.randint(cell_key, (HEADS, NB, NB), 0, 8)
    return (cells < density).astype(jnp.int32)


def head_law(key):
    order_key = jax.random.fold_in(key, 21)
    base_key = jax.random.fold_in(key, 22)
    strong_key = jax.random.fold_in(key, 23)
    temper_key = jax.random.fold_in(key, 24)
    coupling_key = jax.random.fold_in(key, 25)
    ranking = jax.random.permutation(order_key, HEADS)
    strong = ranking < HEADS // 4
    base = jnp.exp(jax.random.uniform(base_key, (3, HEADS), jnp.float32, jnp.log(0.6), jnp.log(2.0)))
    high = jnp.exp(jax.random.uniform(strong_key, (3, HEADS), jnp.float32, jnp.log(5.0), jnp.log(9.0)))
    query_key_rows = (jnp.arange(3, dtype=jnp.int32) < 2)[:, None]
    chosen = jnp.where(query_key_rows & strong[None, :], high, base).astype(jnp.float32)
    temper = jnp.exp(jax.random.uniform(temper_key, (HEADS,), jnp.float32, jnp.log(0.8), jnp.log(2.0)))
    coupling = jax.random.uniform(coupling_key, (HEADS,), jnp.float32, 0.75, 1.0)
    return (chosen, temper, coupling)


def draw_qkv_scale(key, part):
    chosen, temper, coupling = head_law(key)
    return chosen


def draw_w_qkv(key, part):
    chosen, temper, coupling = head_law(key)
    column_gain = jnp.sqrt(temper / (chosen[0] * chosen[1]))
    query_key = jax.random.fold_in(key, 31)
    other_key = jax.random.fold_in(key, 32)
    value_key = jax.random.fold_in(key, 33)
    shape = (D, HEADS * HD)
    query_noise = jax.random.truncated_normal(query_key, -4.0, 4.0, shape, jnp.float32)
    other_noise = jax.random.truncated_normal(other_key, -4.0, 4.0, shape, jnp.float32)
    value_noise = jax.random.truncated_normal(value_key, -4.0, 4.0, shape, jnp.float32)
    head_gain = jnp.repeat(column_gain, HD)[None, :]
    head_coupling = jnp.repeat(coupling, HD)[None, :]
    spread = 1.0 / jnp.sqrt(jnp.float32(D))
    query_cols = head_gain * query_noise * spread
    key_cols = head_gain * (head_coupling * query_noise + jnp.sqrt(1.0 - head_coupling * head_coupling) * other_noise) * spread
    value_cols = value_noise * spread
    return jnp.stack([query_cols, key_cols, value_cols], axis=1).astype(jnp.bfloat16)


def draw_tokens(key, part):
    noise_key = jax.random.fold_in(key, 41)
    direction_key = jax.random.fold_in(key, 42)
    member_key = jax.random.fold_in(key, 43)
    polarity_key = jax.random.fold_in(key, 44)
    strength_key = jax.random.fold_in(key, 45)
    noise = jax.random.truncated_normal(noise_key, -4.0, 4.0, (TOKENS, D), jnp.float32)
    largest = 2.5
    directions = jax.random.truncated_normal(direction_key, -4.0, 4.0, (16, D), jnp.float32)
    member = jax.random.randint(member_key, (TOKENS,), 0, 16)
    polarity = jnp.where(jax.random.randint(polarity_key, (TOKENS,), 0, 2) == 1, 1.0, -1.0)
    strength = jax.random.uniform(strength_key, (TOKENS,), jnp.float32, 0.0, largest)
    shared = jnp.take(directions, member, axis=0)
    return (noise + (polarity * strength)[:, None] * shared).astype(jnp.bfloat16)


def block_scale(stream_key, dims, pieces, low, high):
    loudness, own = 1.0, jax.random.fold_in(stream_key, 6)
    for dim, blocks in pieces:
        heights = jnp.exp(jax.random.uniform(jax.random.fold_in(own, dim), (blocks,), jnp.float32, low / len(pieces), high / len(pieces)))
        loudness = loudness * jnp.repeat(heights, dims[dim] // blocks).reshape([-1 if axis == dim else 1 for axis in range(len(dims))])
    return loudness


def gaussian(stream_key, extent, scale, most, split=(), held_as=jnp.bfloat16):
    result = scale * jax.random.normal(stream_key, extent, jnp.float32)
    if split:
        result = result * block_scale(stream_key, extent, split, -0.22, 0.18)
    return jnp.clip(result, -most, most).astype(held_as)


def setup_inputs(seed: int = 0) -> dict:
    seeds = jax.random.split(jax.random.key(seed), 6)
    return {
        "tokens": draw_tokens(jax.random.fold_in(seeds[5], 71), 0),
        "w_qkv": draw_w_qkv(jax.random.fold_in(seeds[5], 71), 0),
        "qkv_scale": draw_qkv_scale(jax.random.fold_in(seeds[5], 71), 0),
        "block_mask": draw_block_mask(jax.random.fold_in(seeds[5], 71), 0),
        "w_out": gaussian(seeds[4], (N_ULYSSES, N_TENSOR * HPD * HD, D), (HPD * HD * 8) ** -0.5, 0.125, ((1, 4),)),
    }


def attend_head(queries, keys, values, head_mask):
    key_blocks = jnp.arange(TOKENS, dtype=jnp.int32) // BLOCK
    score_scale = 1.0 / math.sqrt(HD)

    def one_block(position):
        query_rows = lax.dynamic_slice_in_dim(queries, (position * BLOCK).astype(jnp.int32), BLOCK, 0)
        scores = jnp.dot(query_rows, keys.T, preferred_element_type=jnp.float32) * score_scale
        allowed = (head_mask[position][key_blocks] == 1) | (key_blocks == position)
        scores = jnp.where(allowed[None, :], scores, -jnp.inf)
        highest = lax.optimization_barrier(jnp.max(scores, axis=-1, keepdims=True))
        weights = jnp.exp(scores - highest)
        denominator = lax.optimization_barrier(jnp.sum(weights, axis=-1, keepdims=True))
        summed = jnp.dot(weights.astype(jnp.bfloat16), values, preferred_element_type=jnp.float32)
        return summed / denominator
    return lax.map(one_block, jnp.arange(NB, dtype=jnp.int32))

def reference(tokens, w_qkv, qkv_scale, block_mask, w_out):
    matrix = w_qkv.reshape(D, 3 * HEADS * HD)
    projected = jnp.dot(tokens, matrix, preferred_element_type=jnp.float32).reshape(TOKENS, 3, HEADS, HD)
    projected = (projected * qkv_scale[None, :, :, None]).astype(jnp.bfloat16)

    def per_head(head_index):
        return attend_head(projected[:, 0, head_index], projected[:, 1, head_index], projected[:, 2, head_index], block_mask[head_index])
    attended = lax.map(per_head, jnp.arange(HEADS, dtype=jnp.int32))
    attended = attended.astype(jnp.bfloat16).reshape(HEADS, TOKENS, HD)
    attended = jnp.transpose(attended, (1, 0, 2)).reshape(TOKENS, HEADS * HD)
    mixed = jnp.dot(attended, w_out.reshape(HEADS * HD, D), preferred_element_type=jnp.float32)
    return mixed.astype(jnp.bfloat16)
```

```python
import functools
import math

import jax
import jax.numpy as jnp
from jax import lax
from jax.experimental import pallas as pl
from jax.experimental.pallas import tpu as pltpu
from jax.sharding import PartitionSpec as P

SUB = 4
F32 = jnp.float32
BF16 = jnp.bfloat16
LOW = -1e30


def by_z(z, zz, s):
    return abs(z - zz) == 1 and s < SUB // 2


def orders(U):
    got = [{(z, s): 0 for s in range(SUB)} for z in range(U)]
    extra = [{} for _ in range(U)]
    for step in (1, -1):
        for a in range(U) if step == 1 else range(U - 1, -1, -1):
            b, free = a + step, 0
            if not 0 <= b < U:
                continue
            zz = a
            while 0 <= zz < U:
                for s in range(SUB):
                    free = max(free, got[a][zz, s]) + 1
                    got[b][zz, s] = free
                zz -= step
            for s in range(SUB // 2):
                free = max(free, s + 1) + 1
                extra[b][a, s] = free
    result = []
    for z in range(U):
        sent = [(z, s) for s in range(SUB)]
        for i in range(SUB * U):
            for zz in (z - 1 - i // SUB, z + 1 + i // SUB):
                if 0 <= zz < U and not by_z(z, zz, i % SUB):
                    sent.append((zz, i % SUB))
        free, done = 0, dict(extra[z])
        for piece in sent:
            free = max(free, got[z][piece]) + 1
            done[piece] = free
        ranked = sorted(done, key=lambda p: (max(done[p], got[z][p]), p))
        result.append([zz * SUB + s for zz, s in ranked])
    return result


def kernel(U, B, T, x_hbm, w_hbm, scale_ref, mask_ref, wo_hbm, out_ref,
           g, w, wo, q, kv, bias, high, den, num, att, arr, part, got, mid, far_got, here,
           w_sem, wo_sem, own_sem,
           zs, zr, up_s, dn_s, du_s, dd_s, xs, xr, cs, cr, fs, fr, ks, kr, as_, ar, ps, pr, ms, mr):
    z, y, t = lax.axis_index("ulysses"), lax.axis_index("blk"), lax.axis_index("tensor")
    near = t + 1 - 2 * lax.rem(t, 2)
    far = lax.rem(t + T // 2, T)
    cross = lax.rem(near + T // 2, T)
    rows, feats = x_hbm.shape
    R = rows // SUB
    H, HD = q.shape[0], q.shape[2]
    N = U * SUB
    NP = N // 2
    R2 = 2 * R
    BR = B * R
    blocks = mask_ref.shape[1]
    nbp = blocks // (U * B)
    block = rows // nbp
    half = SUB // 2

    barrier = pltpu.get_barrier_semaphore()
    for d in range(1, U):
        pl.semaphore_signal(barrier, inc=1, device_id={"ulysses": lax.rem(z + d, U)})
    for d in range(1, B):
        pl.semaphore_signal(barrier, inc=1, device_id={"blk": lax.rem(y + d, B)})
    pl.semaphore_signal(barrier, inc=1, device_id={"tensor": near})
    pl.semaphore_signal(barrier, inc=1, device_id={"tensor": far})

    table = orders(U)
    place = [[order.index(n) for n in range(N)] for order in table]

    def at_z(values):
        out = values[-1]
        for u in range(U - 2, -1, -1):
            out = jnp.where(z == u, values[u], out)
        return out

    slots = [at_z([table[u][n] for u in range(U)]) for n in range(N)]
    places = [at_z([place[u][n] for u in range(U)]) for n in range(N)]

    def pick(values, i):
        out = values[-1]
        for n in range(N - 2, -1, -1):
            out = jnp.where(i == n, values[n], out)
        return out

    def remote(src, dst, send, recv, **where):
        return pltpu.make_async_remote_copy(
            src_ref=src, dst_ref=dst, send_sem=send, recv_sem=recv, device_id=where
        )

    def own_copy(s):
        return pltpu.make_async_copy(x_hbm.at[pl.ds(s * R, R)], g.at[z * SUB + s, t], own_sem.at[s])

    def source(slot, s, own):
        return x_hbm.at[pl.ds(s * R, R)] if own else g.at[slot, t]

    def z_copy(slot, send, target, src=None):
        return remote(g.at[slot, t] if src is None else src, g.at[slot, t], send, zr.at[slot], ulysses=target)

    def x_copy(slot, src=None):
        return remote(g.at[slot, t] if src is None else src, g.at[slot, t], xs.at[slot], xr.at[slot], tensor=far)

    def c_copy(slot, src=None):
        return remote(g.at[slot, t] if src is None else src, g.at[slot, t], cs.at[slot], cr.at[slot], tensor=near)

    def x_arrival(slot):
        return remote(g.at[slot, far], g.at[slot, far], xs.at[slot], xr.at[slot], tensor=far)

    def c_arrival(slot):
        return remote(g.at[slot, near], g.at[slot, near], cs.at[slot], cr.at[slot], tensor=near)

    def f_copy(slot):
        return remote(g.at[slot, far], g.at[slot, far], fs.at[slot], fr.at[slot], tensor=near)

    def f_arrival(slot):
        return remote(g.at[slot, cross], g.at[slot, cross], fs.at[slot], fr.at[slot], tensor=near)

    def d_copy(s, send, target):
        slot = z * SUB + s
        return remote(g.at[slot, far], g.at[slot, far], send, xr.at[slot], ulysses=target)

    def kv_copy(who, i, d):
        view = kv.at[:, :, pl.ds(2 * i, 2), pl.ds(pl.multiple_of(who * R, R), R), :]
        return remote(view, view, ks.at[d - 1, i], kr.at[who, i], blk=lax.rem(y + d, B))

    w_copy = pltpu.make_async_copy(w_hbm, w, w_sem)
    wo_copies = [
        pltpu.make_async_copy(wo_hbm.at[:, :, pl.ds(j * feats, feats)], wo.at[j], wo_sem.at[j])
        for j in range(T)
    ]

    pl.semaphore_wait(barrier, (U - 1) + (B - 1) + 2)

    def own_sends(act):
        for s in range(SUB):
            slot = z * SUB + s
            src = x_hbm.at[pl.ds(s * R, R)]
            act(x_copy(slot, src))

            @pl.when(z + 1 < U)
            def _():
                act(z_copy(slot, up_s.at[s], z + 1, src))

            @pl.when(z > 0)
            def _():
                act(z_copy(slot, dn_s.at[s], z - 1, src))

            act(c_copy(slot, src))

    own_sends(lambda c: c.start())
    for s in range(SUB):
        own_copy(s).start()
    w_copy.start()

    lane = lax.broadcasted_iota(jnp.int32, (1, BR), 1) // R
    key_block = jnp.concatenate(
        [(slots[n] // SUB * B + lane) * nbp + lax.rem(slots[n], SUB) * R // block for n in range(N)], axis=1
    )
    spread = (lax.broadcasted_iota(jnp.int32, (blocks, N * BR), 0) == key_block).astype(F32).astype(BF16)
    ids = lax.broadcasted_iota(jnp.int32, (1, blocks), 1)
    for h in range(H):
        lines = []
        for n in range(N):
            qb = (slots[n] // SUB * B + y) * nbp + lax.rem(slots[n], SUB) * R // block
            lines.append(jnp.where((mask_ref[h, pl.ds(qb, 1), :] == 1) | (ids == qb), 1.0, 0.0))
        allowed = jnp.dot(
            jnp.concatenate(lines, axis=0).astype(BF16), spread, preferred_element_type=F32
        )
        bias[h] = jnp.where(allowed > 0.5, 0.0, -jnp.inf)

    def duplicates(i, act):
        @pl.when((i == jnp.maximum(SUB * z, SUB)) & (z + 1 < U))
        def _():
            for s in range(half):
                act(d_copy(s, du_s.at[s], z + 1))

        @pl.when((i == jnp.maximum(SUB * (U - 1 - z), SUB)) & (z > 0))
        def _():
            for s in range(half):
                act(d_copy(s, dd_s.at[s], z - 1))

    def streams(i, arrive, act):
        s = lax.rem(i, SUB)
        hops = 1 + i // SUB
        crosses = (hops > 1) | (s >= half)
        for step in (1, -1):
            zz = z - step * hops
            slot = zz * SUB + s

            @pl.when((zz >= 0) & (zz < U))
            def _():
                if arrive:
                    z_copy(slot, zs.at[slot], lax.rem(z + 1, U)).wait_recv()

                @pl.when((z + step >= 0) & (z + step < U))
                def _():
                    act(z_copy(slot, zs.at[slot], z + step))

                @pl.when(crosses)
                def _():
                    act(x_copy(slot))

                act(c_copy(slot))

    log2e = 1.4426950408889634
    factor = log2e / math.sqrt(HD)

    def logits(h, qv, q0, nq, k0, nk):
        keys = kv[0, h, pl.ds(k0, nk)].reshape(nk * BR, HD)
        s = lax.dot_general(qv, keys, (((1,), (1,)), ((), ())), preferred_element_type=F32)
        at = pl.ds(pl.multiple_of(k0 * BR, 128), nk * BR)
        return jnp.concatenate(
            [s[r * R:(r + 1) * R] * factor + bias[h, pl.ds(q0 + r, 1), at] for r in range(nq)], axis=0
        )

    def weigh(h, s, new, k0, nk):
        width = nk * BR
        p = jnp.exp2(s - jnp.concatenate([new] * (width // HD), axis=1))
        total = p[:, :HD]
        for j in range(1, width // HD):
            total = total + p[:, j * HD:(j + 1) * HD]
        values = kv[1, h, pl.ds(k0, nk)].reshape(width, HD)
        return total, jnp.dot(p.astype(BF16), values, preferred_element_type=F32)

    def fresh(h, i, nk):
        at = pl.ds(pl.multiple_of(i * R2, R2), R2)
        s = logits(h, q[h, at, :], 2 * i, 2, 0, nk)
        new = jnp.broadcast_to(jnp.maximum(jnp.max(s, axis=1, keepdims=True), LOW), (R2, HD))
        high[h, at, :] = new
        den[h, at, :], num[h, at, :] = weigh(h, s, new, 0, nk)

    def update(h, at, q0, nq, k0, nk):
        s = logits(h, q[h, at, :], q0, nq, k0, nk)
        old = high[h, at, :]
        new = jnp.maximum(old, jnp.max(s, axis=1, keepdims=True))
        total, product = weigh(h, s, new, k0, nk)
        fix = jnp.exp2(old - new)
        return new, den[h, at, :] * fix + total, num[h, at, :] * fix + product

    def older(i):
        def four(j, carry):
            at = pl.ds(pl.multiple_of(j * 4 * R, 4 * R), 4 * R)
            for h in range(H):
                high[h, at, :], den[h, at, :], num[h, at, :] = update(h, at, 4 * j, 4, 2 * i, 2)
            return carry

        lax.fori_loop(0, i // 2, four, 0)

        @pl.when(lax.rem(i, 2) == 1)
        def _():
            at = pl.ds(pl.multiple_of((i - 1) * R2, R2), R2)
            for h in range(H):
                high[h, at, :], den[h, at, :], num[h, at, :] = update(h, at, 2 * (i - 1), 2, 2 * i, 2)

    def kv_wait(i):
        for d in range(1, B):
            kv_copy(lax.rem(y + d, B), i, d).wait_recv()

    def project(i):
        first, second = pick(slots, 2 * i), pick(slots, 2 * i + 1)
        at = pl.ds(pl.multiple_of(i * R2, R2), R2)
        mine = pl.ds(pl.multiple_of(y * R, R), R)
        for c in range(3):
            acc = jnp.zeros((R2, H * HD), F32)
            for k in range(T):
                acc += jnp.dot(
                    jnp.concatenate([g[first, k], g[second, k]], axis=0),
                    w[c, pl.ds(k * feats, feats), :],
                    preferred_element_type=F32,
                )
            for h in range(H):
                val = (acc[:, h * HD:(h + 1) * HD] * scale_ref[h, c]).astype(BF16)
                if c == 0:
                    q[h, at, :] = val
                else:
                    kv[c - 1, h, 2 * i, mine, :] = val[:R]
                    kv[c - 1, h, 2 * i + 1, mine, :] = val[R:]
        for d in range(1, B):
            kv_copy(y, i, d).start()

    def pair(i, carry):
        for e in range(2):
            n = 2 * i + e
            duplicates(n, lambda c: c.start())
            streams(n, True, lambda c: c.start())
            slot = pick(slots, n)
            x_arrival(slot).wait_recv()
            f_copy(slot).start()

        @pl.when(i == 0)
        def _():
            w_copy.wait()
            for s in range(SUB):
                own_copy(s).wait()

        @pl.when(i == 1)
        def _():
            for c in wo_copies:
                c.start()

        for e in range(2):
            slot = pick(slots, 2 * i + e)
            c_arrival(slot).wait_recv()
            f_arrival(slot).wait_recv()
        project(i)

        @pl.when(i > 0)
        def _():
            kv_wait(i - 1)
            older(i - 1)

        for k in range(NP - 1):
            @pl.when(i == k + 1)
            def _():
                for h in range(H):
                    fresh(h, k, 2 * (k + 1))

        return carry

    lax.fori_loop(0, NP, pair, 0)
    for h in range(H):
        fresh(h, NP - 1, 2 * (NP - 1))
    kv_wait(NP - 1)

    def a_copy(c, zz, src):
        at = pl.ds(pl.multiple_of(c * R, R), R)
        return remote(att.at[zz, at], arr.at[src, at], as_.at[zz, c], ar.at[src, c], ulysses=zz)

    def finish(c, carry):
        at = pl.ds(pl.multiple_of(c * R, R), R)
        for d in range(U - 1, -1, -1):
            zz = lax.rem(z + d, U)
            n = pick(places, zz * SUB + c)
            from_ = pl.ds(pl.multiple_of(n * R, R), R)
            for h in range(H):
                _, total, product = update(h, from_, n, 1, 2 * (NP - 1), 2)
                val = (product / jnp.sum(total, axis=1, keepdims=True)).astype(BF16)
                if d == 0:
                    arr[z, at, h * HD:(h + 1) * HD] = val
                else:
                    att[zz, at, h * HD:(h + 1) * HD] = val
        for d in range(U - 1, 0, -1):
            zz = lax.rem(z + d, U)
            a_copy(c, zz, z).start()
        return carry

    lax.fori_loop(0, SUB, finish, 0)
    for c in wo_copies:
        c.wait()

    def product(c, col):
        at = pl.ds(pl.multiple_of(c * R, R), R)
        acc = jnp.dot(arr[0, at, :], wo[col, 0], preferred_element_type=F32)
        for u in range(1, U):
            acc += jnp.dot(arr[u, at, :], wo[col, u], preferred_element_type=F32)
        return acc

    def p_copy(k, c):
        at = pl.ds(pl.multiple_of(c * R, R), R)
        return remote(part.at[k, at], got.at[k, at], ps.at[k, c], pr.at[k, c], tensor=near)

    def m_copy(c):
        at = pl.ds(pl.multiple_of(c * R, R), R)
        return remote(mid.at[at], far_got.at[at], ms.at[c], mr.at[c], tensor=far)

    def outward(c, carry):
        at = pl.ds(pl.multiple_of(c * R, R), R)
        for d in range(1, U):
            zz = lax.rem(z + d, U)
            a_copy(c, zz, zz).wait_recv()
        part[0, at] = product(c, cross).astype(BF16)
        p_copy(0, c).start()
        there = product(c, far)
        p_copy(0, c).wait_recv()
        mid[at] = (there + got[0, at].astype(F32)).astype(BF16)
        m_copy(c).start()
        return carry

    lax.fori_loop(0, SUB, outward, 0)

    def inward(c, carry):
        at = pl.ds(pl.multiple_of(c * R, R), R)
        part[1, at] = product(c, near).astype(BF16)
        p_copy(1, c).start()
        here[at] = product(c, t)
        return carry

    lax.fori_loop(0, SUB, inward, 0)

    def total(c, carry):
        at = pl.ds(pl.multiple_of(c * R, R), R)
        p_copy(1, c).wait_recv()
        near_sum = here[at] + got[1, at].astype(F32)
        m_copy(c).wait_recv()
        out_ref[at] = (near_sum + far_got[at].astype(F32)).astype(BF16)
        return carry

    lax.fori_loop(0, SUB, total, 0)

    own_sends(lambda c: c.wait_send())

    def drain(i, carry):
        duplicates(i, lambda c: c.wait_send())
        streams(i, False, lambda c: c.wait_send())
        f_copy(i).wait_send()
        return carry

    lax.fori_loop(0, N, drain, 0)

    def kv_drain(i, carry):
        for d in range(1, B):
            kv_copy(y, i, d).wait_send()
        return carry

    lax.fori_loop(0, NP, kv_drain, 0)

    def out_drain(c, carry):
        for d in range(1, U):
            a_copy(c, lax.rem(z + d, U), z).wait_send()
        p_copy(0, c).wait_send()
        p_copy(1, c).wait_send()
        m_copy(c).wait_send()
        return carry

    lax.fori_loop(0, SUB, out_drain, 0)


def local(tokens, w_qkv, qkv_scale, block_mask, w_out):
    U, B, T = lax.axis_size("ulysses"), lax.axis_size("blk"), lax.axis_size("tensor")
    rows, feats = tokens.shape
    heads = block_mask.shape[0]
    cols = w_qkv.shape[2]
    hd = cols // heads
    R, N = rows // SUB, U * SUB
    dma = lambda *s: pltpu.SemaphoreType.DMA(s)
    vmem = pl.BlockSpec(memory_space=pltpu.VMEM)
    hbm = pl.BlockSpec(memory_space=pl.ANY)
    return pl.pallas_call(
        functools.partial(kernel, U, B, T),
        out_shape=jax.ShapeDtypeStruct((rows, feats), BF16),
        in_specs=[hbm, hbm, pl.BlockSpec(memory_space=pltpu.SMEM), vmem, hbm],
        out_specs=vmem,
        scratch_shapes=[
            pltpu.VMEM((N, T, R, feats), BF16),
            pltpu.VMEM((3, T * feats, cols), BF16),
            pltpu.VMEM((T, U, cols, feats), BF16),
            pltpu.VMEM((heads, U * rows, hd), BF16),
            pltpu.VMEM((2, heads, N, B * R, hd), BF16),
            pltpu.VMEM((heads, N, N * B * R), F32),
            pltpu.VMEM((heads, U * rows, hd), F32),
            pltpu.VMEM((heads, U * rows, hd), F32),
            pltpu.VMEM((heads, U * rows, hd), F32),
            pltpu.VMEM((U, rows, cols), BF16),
            pltpu.VMEM((U, rows, cols), BF16),
            pltpu.VMEM((2, rows, feats), BF16),
            pltpu.VMEM((2, rows, feats), BF16),
            pltpu.VMEM((rows, feats), BF16),
            pltpu.VMEM((rows, feats), BF16),
            pltpu.VMEM((rows, feats), F32),
            pltpu.SemaphoreType.DMA,
            dma(T),
            dma(SUB),
            dma(N), dma(N), dma(SUB), dma(SUB), dma(SUB), dma(SUB),
            dma(N), dma(N), dma(N), dma(N), dma(N), dma(N),
            dma(B, N // 2), dma(B, N // 2),
            dma(U, SUB), dma(U, SUB),
            dma(2, SUB), dma(2, SUB),
            dma(SUB), dma(SUB),
        ],
        compiler_params=pltpu.CompilerParams(
            collective_id=0, has_side_effects=True, vmem_limit_bytes=62 * 1024 * 1024
        ),
    )(tokens, jnp.transpose(w_qkv, (1, 0, 2)), qkv_scale.T, block_mask, w_out)


def solution(mesh):
    return jax.shard_map(
        local,
        mesh=mesh,
        in_specs=(
            P(("ulysses", "blk"), "tensor"),
            P(None, None, ("ulysses", "tensor")),
            P(None, ("ulysses", "tensor")),
            P(("ulysses", "tensor"), None, None),
            P(None, "tensor", None),
        ),
        out_specs=P(("ulysses", "blk"), "tensor"),
        check_vma=False,
    )
```

```python
import functools
import math

import jax
import jax.numpy as jnp
from jax import lax
from jax.experimental import pallas as pl
from jax.experimental.pallas import tpu as pltpu
from jax.sharding import PartitionSpec as P

SUB = 4
PARTS = 8
WIDE = 2
F32 = jnp.float32
BF16 = jnp.bfloat16
LOW = -1e30


def by_z(z, zz, s):
    return abs(z - zz) == 1 and s < SUB // 2


def orders(U):
    got = [{(z, s): 0 for s in range(SUB)} for z in range(U)]
    extra = [{} for _ in range(U)]
    for step in (1, -1):
        for a in range(U) if step == 1 else range(U - 1, -1, -1):
            b, free = a + step, 0
            if not 0 <= b < U:
                continue
            zz = a
            while 0 <= zz < U:
                for s in range(SUB):
                    free = max(free, got[a][zz, s]) + 1
                    got[b][zz, s] = free
                zz -= step
            for s in range(SUB // 2):
                free = max(free, s + 1) + 1
                extra[b][a, s] = free
    result = []
    for z in range(U):
        sent = [(z, s) for s in range(SUB)]
        for i in range(SUB * U):
            for zz in (z - 1 - i // SUB, z + 1 + i // SUB):
                if 0 <= zz < U and not by_z(z, zz, i % SUB):
                    sent.append((zz, i % SUB))
        free, done = 0, dict(extra[z])
        for piece in sent:
            free = max(free, got[z][piece]) + 1
            done[piece] = free
        ranked = sorted(done, key=lambda p: (max(done[p], got[z][p]), p))
        result.append([zz * SUB + s for zz, s in ranked])
    return result


def kernel(U, B, T, x_hbm, w_hbm, scale_hbm, mask_hbm, wo_hbm, near_out, far_out,
           g, w, wo, q, kv, bias, high, den, num, att, arr, part, got, back, back_got, mid, here, sums,
           scale_ref, mask_ref, small_sem,
           w_sem, wo_sem, own_sem,
           zs, zr, up_s, dn_s, du_s, dd_s, xs, xr, cs, cr, fs, fr, ks, kr, as_, ar, ps, pr, bs, br, ms, mr, hs):
    z, y, t = lax.axis_index("ulysses"), lax.axis_index("blk"), lax.axis_index("tensor")
    near = t + 1 - 2 * lax.rem(t, 2)
    far = lax.rem(t + T // 2, T)
    cross = lax.rem(near + T // 2, T)
    rows, feats = x_hbm.shape
    R = rows // SUB
    H, HD = q.shape[0], q.shape[2]
    N = U * SUB
    NP = N // 2
    R2 = 2 * R
    BR = B * R
    blocks = mask_ref.shape[1]
    nbp = blocks // (U * B)
    block = rows // nbp
    half = SUB // 2

    barrier = pltpu.get_barrier_semaphore()
    for d in range(1, U):
        pl.semaphore_signal(barrier, inc=1, device_id={"ulysses": lax.rem(z + d, U)})
    for d in range(1, B):
        pl.semaphore_signal(barrier, inc=1, device_id={"blk": lax.rem(y + d, B)})
    pl.semaphore_signal(barrier, inc=1, device_id={"tensor": near})
    pl.semaphore_signal(barrier, inc=1, device_id={"tensor": far})

    table = orders(U)
    place = [[order.index(n) for n in range(N)] for order in table]

    def at_z(values):
        out = values[-1]
        for u in range(U - 2, -1, -1):
            out = jnp.where(z == u, values[u], out)
        return out

    slots = [at_z([table[u][n] for u in range(U)]) for n in range(N)]
    places = [at_z([place[u][n] for u in range(U)]) for n in range(N)]

    def pick(values, i):
        out = values[-1]
        for n in range(N - 2, -1, -1):
            out = jnp.where(i == n, values[n], out)
        return out

    def remote(src, dst, send, recv, **where):
        return pltpu.make_async_remote_copy(
            src_ref=src, dst_ref=dst, send_sem=send, recv_sem=recv, device_id=where
        )

    def own_copy(s):
        return pltpu.make_async_copy(x_hbm.at[pl.ds(s * R, R)], g.at[z * SUB + s, t], own_sem.at[s])

    def source(slot, s, own):
        return x_hbm.at[pl.ds(s * R, R)] if own else g.at[slot, t]

    def z_copy(slot, send, target, src=None):
        return remote(g.at[slot, t] if src is None else src, g.at[slot, t], send, zr.at[slot], ulysses=target)

    def x_copy(slot, src=None):
        return remote(g.at[slot, t] if src is None else src, g.at[slot, t], xs.at[slot], xr.at[slot], tensor=far)

    def c_copy(slot, src=None):
        return remote(g.at[slot, t] if src is None else src, g.at[slot, t], cs.at[slot], cr.at[slot], tensor=near)

    def x_arrival(slot):
        return remote(g.at[slot, far], g.at[slot, far], xs.at[slot], xr.at[slot], tensor=far)

    def c_arrival(slot):
        return remote(g.at[slot, near], g.at[slot, near], cs.at[slot], cr.at[slot], tensor=near)

    def f_copy(slot):
        return remote(g.at[slot, far], g.at[slot, far], fs.at[slot], fr.at[slot], tensor=near)

    def f_arrival(slot):
        return remote(g.at[slot, cross], g.at[slot, cross], fs.at[slot], fr.at[slot], tensor=near)

    def d_copy(s, send, target):
        slot = z * SUB + s
        return remote(g.at[slot, far], g.at[slot, far], send, xr.at[slot], ulysses=target)

    def kv_copy(who, i, h, d):
        view = kv.at[:, h, pl.ds(2 * i, 2), pl.ds(pl.multiple_of(who * R, R), R), :]
        return remote(view, view, ks.at[d - 1, i, h], kr.at[who, i, h], blk=lax.rem(y + d, B))

    w_copy = pltpu.make_async_copy(w_hbm, w, w_sem)
    wo_copies = [
        pltpu.make_async_copy(wo_hbm.at[:, :, pl.ds(j * feats, feats)], wo.at[j], wo_sem.at[j])
        for j in range(T)
    ]

    small = [
        pltpu.make_async_copy(scale_hbm, scale_ref, small_sem.at[0]),
        pltpu.make_async_copy(mask_hbm, mask_ref, small_sem.at[1]),
    ]
    for c in small:
        c.start()

    pl.semaphore_wait(barrier, (U - 1) + (B - 1) + 2)

    def own_sends(act):
        for s in range(SUB):
            slot = z * SUB + s
            src = x_hbm.at[pl.ds(s * R, R)]
            act(x_copy(slot, src))

            @pl.when(z + 1 < U)
            def _():
                act(z_copy(slot, up_s.at[s], z + 1, src))

            @pl.when(z > 0)
            def _():
                act(z_copy(slot, dn_s.at[s], z - 1, src))

            act(c_copy(slot, src))

    own_sends(lambda c: c.start())
    for s in range(SUB):
        own_copy(s).start()
    w_copy.start()
    for c in small:
        c.wait()

    lane = lax.broadcasted_iota(jnp.int32, (1, BR), 1) // R
    key_block = jnp.concatenate(
        [(slots[n] // SUB * B + lane) * nbp + lax.rem(slots[n], SUB) * R // block for n in range(N)], axis=1
    )
    spread = (lax.broadcasted_iota(jnp.int32, (blocks, N * BR), 0) == key_block).astype(F32).astype(BF16)
    ids = lax.broadcasted_iota(jnp.int32, (1, blocks), 1)
    for h in range(H):
        lines = []
        for n in range(N):
            qb = (slots[n] // SUB * B + y) * nbp + lax.rem(slots[n], SUB) * R // block
            lines.append(jnp.where((mask_ref[h, pl.ds(qb, 1), :] == 1) | (ids == qb), 1.0, 0.0))
        allowed = jnp.dot(
            jnp.concatenate(lines, axis=0).astype(BF16), spread, preferred_element_type=F32
        )
        bias[h] = jnp.where(allowed > 0.5, 0.0, -jnp.inf)

    def duplicates(i, act):
        @pl.when((i == jnp.maximum(SUB * z, SUB)) & (z + 1 < U))
        def _():
            for s in range(half):
                act(d_copy(s, du_s.at[s], z + 1))

        @pl.when((i == jnp.maximum(SUB * (U - 1 - z), SUB)) & (z > 0))
        def _():
            for s in range(half):
                act(d_copy(s, dd_s.at[s], z - 1))

    def streams(i, arrive, act):
        s = lax.rem(i, SUB)
        hops = 1 + i // SUB
        crosses = (hops > 1) | (s >= half)
        for step in (1, -1):
            zz = z - step * hops
            slot = zz * SUB + s

            @pl.when((zz >= 0) & (zz < U))
            def _():
                if arrive:
                    z_copy(slot, zs.at[slot], lax.rem(z + 1, U)).wait_recv()

                @pl.when((z + step >= 0) & (z + step < U))
                def _():
                    act(z_copy(slot, zs.at[slot], z + step))

                @pl.when(crosses)
                def _():
                    act(x_copy(slot))

                act(c_copy(slot))

    log2e = 1.4426950408889634
    factor = log2e / math.sqrt(HD)

    def logits(h, qv, q0, nq, k0, nk):
        keys = kv[0, h, pl.ds(k0, nk)].reshape(nk * BR, HD)
        s = lax.dot_general(qv, keys, (((1,), (1,)), ((), ())), preferred_element_type=F32)
        at = pl.ds(pl.multiple_of(k0 * BR, 128), nk * BR)
        return jnp.concatenate(
            [s[r * R:(r + 1) * R] * factor + bias[h, pl.ds(q0 + r, 1), at] for r in range(nq)], axis=0
        )

    def weigh(h, s, new, k0, nk):
        width = nk * BR
        p = jnp.exp2(s - jnp.concatenate([new] * (width // HD), axis=1))
        total = p[:, :HD]
        for j in range(1, width // HD):
            total = total + p[:, j * HD:(j + 1) * HD]
        values = kv[1, h, pl.ds(k0, nk)].reshape(width, HD)
        return total, jnp.dot(p.astype(BF16), values, preferred_element_type=F32)

    def fresh(h, i, nk):
        at = pl.ds(pl.multiple_of(i * R2, R2), R2)
        s = logits(h, q[h, at, :], 2 * i, 2, 0, nk)
        new = jnp.broadcast_to(jnp.maximum(jnp.max(s, axis=1, keepdims=True), LOW), (R2, HD))
        high[h, at, :] = new
        den[h, at, :], num[h, at, :] = weigh(h, s, new, 0, nk)

    def update(h, at, q0, nq, k0, nk):
        s = logits(h, q[h, at, :], q0, nq, k0, nk)
        old = high[h, at, :]
        new = jnp.maximum(old, jnp.max(s, axis=1, keepdims=True))
        total, product = weigh(h, s, new, k0, nk)
        fix = jnp.exp2(old - new)
        return new, den[h, at, :] * fix + total, num[h, at, :] * fix + product

    def attend(k):
        for h in range(H):
            if k > 0:
                at = pl.ds(0, k * R2)
                high[h, at, :], den[h, at, :], num[h, at, :] = update(h, at, 0, 2 * k, 2 * k, 2)
            fresh(h, k, 2 * (k + 1))

    def kv_wait(i, h):
        for d in range(1, B):
            kv_copy(lax.rem(y + d, B), i, h, d).wait_recv()

    def project(i):
        first, second = pick(slots, 2 * i), pick(slots, 2 * i + 1)
        at = pl.ds(pl.multiple_of(i * R2, R2), R2)
        mine = pl.ds(pl.multiple_of(y * R, R), R)

        def term(c, k):
            return jnp.dot(
                jnp.concatenate([g[first, k], g[second, k]], axis=0),
                w[c, pl.ds(pl.multiple_of(k * feats, feats), feats), :],
                preferred_element_type=F32,
            )

        for slot in (first, second):
            c_arrival(slot).wait_recv()
        for c in range(3):
            sums[c] = term(c, t) + term(c, near) + term(c, far)
        for slot in (first, second):
            f_arrival(slot).wait_recv()
        for c in (1, 2, 0):
            acc = sums[c] + term(c, cross)
            for h in range(H):
                val = (acc[:, h * HD:(h + 1) * HD] * scale_ref[h, c]).astype(BF16)
                if c == 0:
                    q[h, at, :] = val
                else:
                    kv[c - 1, h, 2 * i, mine, :] = val[:R]
                    kv[c - 1, h, 2 * i + 1, mine, :] = val[R:]
                if c == 2:
                    for d in range(1, B):
                        kv_copy(y, i, h, d).start()

    def pair(i, carry):
        for e in range(2):
            n = 2 * i + e
            duplicates(n, lambda c: c.start())
            streams(n, True, lambda c: c.start())
            slot = pick(slots, n)
            x_arrival(slot).wait_recv()
            f_copy(slot).start()

        @pl.when(i == 0)
        def _():
            w_copy.wait()
            for s in range(SUB):
                own_copy(s).wait()

        @pl.when(i == 1)
        def _():
            for c in wo_copies:
                c.start()

        project(i)

        for k in range(NP - 1):
            @pl.when(i == k + 1)
            def _():
                for h in range(H):
                    kv_wait(k, h)
                attend(k)

        return carry

    lax.fori_loop(0, NP, pair, 0)
    for h in range(H):
        fresh(h, NP - 1, 2 * (NP - 1))
    RC = rows // PARTS
    RW = rows // WIDE
    per = PARTS // SUB

    def chunk(c, size=RC):
        return pl.ds(pl.multiple_of(c * size, size), size)

    def at_place(zz, c):
        first = pick(places, zz * SUB + c // per) * R + lax.rem(c, per) * RC
        return pl.ds(pl.multiple_of(first, RC), RC)

    def a_copy(c, h, zz, src):
        return remote(
            att.at[h, at_place(zz, c)],
            arr.at[src, chunk(c), pl.ds(h * HD, HD)],
            as_.at[zz, c, h],
            ar.at[src, c, h],
            ulysses=zz,
        )

    def spread_out(c, h):
        for d in range(U - 1, 0, -1):
            a_copy(c, h, lax.rem(z + d, U), z).start()

    for h in range(H):
        kv_wait(NP - 1, h)
        _, weight, value = update(h, pl.ds(0, N * R), 0, N, 2 * (NP - 1), 2)
        att[h] = (value / jnp.sum(weight, axis=1, keepdims=True)).astype(BF16)
        if h < H - 1:
            spread_out(0, h)

    def spread_rest(c, carry):
        spread_out(c, H - 1)

        @pl.when(c + 1 < PARTS)
        def _():
            for h in range(H - 1):
                spread_out(c + 1, h)

        for h in range(H):
            arr[z, chunk(c), h * HD:(h + 1) * HD] = att[h, at_place(z, c), :]
        return carry

    lax.fori_loop(0, PARTS, spread_rest, 0)
    for c in wo_copies:
        c.wait()

    def product(at, col):
        acc = jnp.dot(arr[0, at, :], wo[col, 0], preferred_element_type=F32)
        for u in range(1, U):
            acc += jnp.dot(arr[u, at, :], wo[col, u], preferred_element_type=F32)
        return acc

    def p_copy(c):
        return remote(part.at[chunk(c)], got.at[chunk(c)], ps.at[c], pr.at[c], tensor=near)

    def b_copy(c):
        at = chunk(c, RW)
        return remote(back.at[at], back_got.at[at], bs.at[c], br.at[c], tensor=near)

    def m_copy(c):
        return remote(mid.at[chunk(c)], far_out.at[chunk(c)], ms.at[c], mr.at[c], tensor=far)

    def h_copy(c):
        return pltpu.make_async_copy(here.at[chunk(c, RW)], near_out.at[chunk(c, RW)], hs.at[c])

    def lead(c):
        at = chunk(c)
        for d in range(1, U):
            for h in range(H):
                zz = lax.rem(z + d, U)
                a_copy(c, h, zz, zz).wait_recv()
        part[at] = product(at, cross).astype(BF16)
        p_copy(c).start()

    def follow(c):
        at = chunk(c)
        there = product(at, far)
        p_copy(c).wait_recv()
        mid[at] = (there + got[at].astype(F32)).astype(BF16)
        m_copy(c).start()

    def outward(c, carry):
        lead(c + 1)
        follow(c)
        return carry

    lead(0)
    follow(0)
    lead(1)
    lax.fori_loop(1, PARTS - 1, outward, 0)
    follow(PARTS - 1)

    for c in range(WIDE):
        at = chunk(c, RW)
        back[at] = product(at, near).astype(BF16)
        b_copy(c).start()
        here[at] = product(at, t)
    for c in range(WIDE):
        at = chunk(c, RW)
        b_copy(c).wait_recv()
        here[at] = here[at] + back_got[at].astype(F32)
        h_copy(c).start()

    own_sends(lambda c: c.wait_send())

    def drain(i, carry):
        duplicates(i, lambda c: c.wait_send())
        streams(i, False, lambda c: c.wait_send())
        f_copy(i).wait_send()
        return carry

    lax.fori_loop(0, N, drain, 0)

    def kv_drain(i, carry):
        for h in range(H):
            for d in range(1, B):
                kv_copy(y, i, h, d).wait_send()
        return carry

    lax.fori_loop(0, NP, kv_drain, 0)

    def out_drain(c, carry):
        for d in range(1, U):
            for h in range(H):
                a_copy(c, h, lax.rem(z + d, U), z).wait_send()
        p_copy(c).wait_send()
        m_copy(c).wait_send()
        m_copy(c).wait_recv()
        return carry

    lax.fori_loop(0, PARTS, out_drain, 0)
    for c in range(WIDE):
        b_copy(c).wait_send()
        h_copy(c).wait()


def local(tokens, w_qkv, qkv_scale, block_mask, w_out):
    U, B, T = lax.axis_size("ulysses"), lax.axis_size("blk"), lax.axis_size("tensor")
    rows, feats = tokens.shape
    heads = block_mask.shape[0]
    cols = w_qkv.shape[2]
    hd = cols // heads
    R, N = rows // SUB, U * SUB
    dma = lambda *s: pltpu.SemaphoreType.DMA(s)
    near_sum, far_sum = pl.pallas_call(
        functools.partial(kernel, U, B, T),
        out_shape=(jax.ShapeDtypeStruct((rows, feats), F32), jax.ShapeDtypeStruct((rows, feats), BF16)),
        in_specs=[pl.BlockSpec(memory_space=pltpu.HBM)] * 5,
        out_specs=(pl.BlockSpec(memory_space=pl.ANY),) * 2,
        scratch_shapes=[
            pltpu.VMEM((N, T, R, feats), BF16),
            pltpu.VMEM((3, T * feats, cols), BF16),
            pltpu.VMEM((T, U, cols, feats), BF16),
            pltpu.VMEM((heads, U * rows, hd), BF16),
            pltpu.VMEM((2, heads, N, B * R, hd), BF16),
            pltpu.VMEM((heads, N, N * B * R), F32),
            pltpu.VMEM((heads, U * rows, hd), F32),
            pltpu.VMEM((heads, U * rows, hd), F32),
            pltpu.VMEM((heads, U * rows, hd), F32),
            pltpu.VMEM((heads, U * rows, hd), BF16),
            pltpu.VMEM((U, rows, cols), BF16),
            pltpu.VMEM((rows, feats), BF16),
            pltpu.VMEM((rows, feats), BF16),
            pltpu.VMEM((rows, feats), BF16),
            pltpu.VMEM((rows, feats), BF16),
            pltpu.VMEM((rows, feats), BF16),
            pltpu.VMEM((rows, feats), F32),
            pltpu.VMEM((3, 2 * R, cols), F32),
            pltpu.SMEM(qkv_scale.T.shape, F32),
            pltpu.VMEM(block_mask.shape, jnp.int32),
            dma(2),
            pltpu.SemaphoreType.DMA,
            dma(T),
            dma(SUB),
            dma(N), dma(N), dma(SUB), dma(SUB), dma(SUB), dma(SUB),
            dma(N), dma(N), dma(N), dma(N), dma(N), dma(N),
            dma(B, N // 2, heads), dma(B, N // 2, heads),
            dma(U, PARTS, heads), dma(U, PARTS, heads),
            dma(PARTS), dma(PARTS), dma(WIDE), dma(WIDE), dma(PARTS), dma(PARTS), dma(WIDE),
        ],
        compiler_params=pltpu.CompilerParams(
            collective_id=0, has_side_effects=True, vmem_limit_bytes=62 * 1024 * 1024
        ),
    )(tokens, jnp.transpose(w_qkv, (1, 0, 2)), qkv_scale.T, block_mask, w_out)
    return (near_sum + far_sum.astype(F32)).astype(BF16)


def solution(mesh):
    return jax.shard_map(
        local,
        mesh=mesh,
        in_specs=(
            P(("ulysses", "blk"), "tensor"),
            P(None, None, ("ulysses", "tensor")),
            P(None, ("ulysses", "tensor")),
            P(("ulysses", "tensor"), None, None),
            P(None, "tensor", None),
        ),
        out_specs=P(("ulysses", "blk"), "tensor"),
        check_vma=False,
    )
```

```python
import functools
import math

import jax
import jax.numpy as jnp
from jax import lax
from jax.experimental import pallas as pl
from jax.experimental.pallas import tpu as pltpu
from jax.sharding import PartitionSpec as P

SUB = 4
PARTS = 8
WIDE = 2
F32 = jnp.float32
BF16 = jnp.bfloat16
LOW = -1e30


def by_z(z, zz, s):
    return abs(z - zz) == 1 and s < SUB // 2


def orders(U):
    got = [{(z, s): 0 for s in range(SUB)} for z in range(U)]
    extra = [{} for _ in range(U)]
    for step in (1, -1):
        for a in range(U) if step == 1 else range(U - 1, -1, -1):
            b, free = a + step, 0
            if not 0 <= b < U:
                continue
            zz = a
            while 0 <= zz < U:
                for s in range(SUB):
                    free = max(free, got[a][zz, s]) + 1
                    got[b][zz, s] = free
                zz -= step
            for s in range(SUB // 2):
                free = max(free, s + 1) + 1
                extra[b][a, s] = free
    result = []
    for z in range(U):
        sent = [(z, s) for s in range(SUB)]
        for i in range(SUB * U):
            for zz in (z - 1 - i // SUB, z + 1 + i // SUB):
                if 0 <= zz < U and not by_z(z, zz, i % SUB):
                    sent.append((zz, i % SUB))
        free, done = 0, dict(extra[z])
        for piece in sent:
            free = max(free, got[z][piece]) + 1
            done[piece] = free
        ranked = sorted(done, key=lambda p: (max(done[p], got[z][p]), p))
        result.append([zz * SUB + s for zz, s in ranked])
    return result


def kernel(U, B, T, x_hbm, w_hbm, scale_hbm, mask_hbm, wo_hbm, near_out, far_out,
           g, w, wo, q, kv, bias, high, den, num, att, arr, part, got, back, back_got, mid, here, sums,
           scale_ref, mask_ref, small_sem,
           w_sem, wo_sem, own_sem,
           zs, zr, up_s, dn_s, du_s, dd_s, xs, xr, cs, cr, fs, fr, ks, kr, as_, ar, ps, pr, bs, br, ms, mr, hs):
    z, y, t = lax.axis_index("ulysses"), lax.axis_index("blk"), lax.axis_index("tensor")
    near = t + 1 - 2 * lax.rem(t, 2)
    far = lax.rem(t + T // 2, T)
    cross = lax.rem(near + T // 2, T)
    rows, feats = x_hbm.shape
    R = rows // SUB
    H, HD = q.shape[0], q.shape[2]
    N = U * SUB
    NP = N // 2
    R2 = 2 * R
    BR = B * R
    blocks = mask_ref.shape[1]
    nbp = blocks // (U * B)
    block = rows // nbp
    half = SUB // 2

    barrier = pltpu.get_barrier_semaphore()
    for step in (1, -1):
        @pl.when((z + step >= 0) & (z + step < U))
        def _():
            pl.semaphore_signal(barrier, inc=1, device_id={"ulysses": z + step})
    for d in range(1, B):
        pl.semaphore_signal(barrier, inc=1, device_id={"blk": lax.rem(y + d, B)})
    pl.semaphore_signal(barrier, inc=1, device_id={"tensor": near})
    pl.semaphore_signal(barrier, inc=1, device_id={"tensor": far})

    table = orders(U)
    place = [[order.index(n) for n in range(N)] for order in table]

    def at_z(values):
        out = values[-1]
        for u in range(U - 2, -1, -1):
            out = jnp.where(z == u, values[u], out)
        return out

    slots = [at_z([table[u][n] for u in range(U)]) for n in range(N)]
    places = [at_z([place[u][n] for u in range(U)]) for n in range(N)]

    def pick(values, i):
        out = values[-1]
        for n in range(N - 2, -1, -1):
            out = jnp.where(i == n, values[n], out)
        return out

    def remote(src, dst, send, recv, **where):
        return pltpu.make_async_remote_copy(
            src_ref=src, dst_ref=dst, send_sem=send, recv_sem=recv, device_id=where
        )

    def own_copy(s):
        return pltpu.make_async_copy(x_hbm.at[pl.ds(s * R, R)], g.at[z * SUB + s, t], own_sem.at[s])

    def source(slot, s, own):
        return x_hbm.at[pl.ds(s * R, R)] if own else g.at[slot, t]

    def z_copy(slot, send, target, src=None):
        return remote(g.at[slot, t] if src is None else src, g.at[slot, t], send, zr.at[slot], ulysses=target)

    def x_copy(slot, src=None):
        return remote(g.at[slot, t] if src is None else src, g.at[slot, t], xs.at[slot], xr.at[slot], tensor=far)

    def c_copy(slot, src=None):
        return remote(g.at[slot, t] if src is None else src, g.at[slot, t], cs.at[slot], cr.at[slot], tensor=near)

    def x_arrival(slot):
        return remote(g.at[slot, far], g.at[slot, far], xs.at[slot], xr.at[slot], tensor=far)

    def c_arrival(slot):
        return remote(g.at[slot, near], g.at[slot, near], cs.at[slot], cr.at[slot], tensor=near)

    def f_copy(slot):
        return remote(g.at[slot, far], g.at[slot, far], fs.at[slot], fr.at[slot], tensor=near)

    def f_arrival(slot):
        return remote(g.at[slot, cross], g.at[slot, cross], fs.at[slot], fr.at[slot], tensor=near)

    def d_copy(s, send, target):
        slot = z * SUB + s
        return remote(g.at[slot, far], g.at[slot, far], send, xr.at[slot], ulysses=target)

    def kv_copy(who, i, h, d):
        view = kv.at[:, h, pl.ds(2 * i, 2), pl.ds(pl.multiple_of(who * R, R), R), :]
        return remote(view, view, ks.at[d - 1, i, h], kr.at[who, i, h], blk=lax.rem(y + d, B))

    w_copy = pltpu.make_async_copy(w_hbm, w, w_sem)
    wo_copies = [
        pltpu.make_async_copy(wo_hbm.at[:, :, pl.ds(j * feats, feats)], wo.at[j], wo_sem.at[j])
        for j in range(T)
    ]

    small = [
        pltpu.make_async_copy(scale_hbm, scale_ref, small_sem.at[0]),
        pltpu.make_async_copy(mask_hbm, mask_ref, small_sem.at[1]),
    ]
    for c in small:
        c.start()

    sides = jnp.where(z > 0, 1, 0) + jnp.where(z + 1 < U, 1, 0)
    pl.semaphore_wait(barrier, sides + (B - 1) + 2)

    def own_sends(act):
        for s in range(SUB):
            slot = z * SUB + s
            src = x_hbm.at[pl.ds(s * R, R)]
            act(x_copy(slot, src))

            @pl.when(z + 1 < U)
            def _():
                act(z_copy(slot, up_s.at[s], z + 1, src))

            @pl.when(z > 0)
            def _():
                act(z_copy(slot, dn_s.at[s], z - 1, src))

            act(c_copy(slot, src))

    own_sends(lambda c: c.start())
    for s in range(SUB):
        own_copy(s).start()
    w_copy.start()
    for c in small:
        c.wait()

    lane = lax.broadcasted_iota(jnp.int32, (1, BR), 1) // R
    key_block = jnp.concatenate(
        [(slots[n] // SUB * B + lane) * nbp + lax.rem(slots[n], SUB) * R // block for n in range(N)], axis=1
    )
    spread = (lax.broadcasted_iota(jnp.int32, (blocks, N * BR), 0) == key_block).astype(F32).astype(BF16)
    ids = lax.broadcasted_iota(jnp.int32, (1, blocks), 1)
    for h in range(H):
        lines = []
        for n in range(N):
            qb = (slots[n] // SUB * B + y) * nbp + lax.rem(slots[n], SUB) * R // block
            lines.append(jnp.where((mask_ref[h, pl.ds(qb, 1), :] == 1) | (ids == qb), 1.0, 0.0))
        allowed = jnp.dot(
            jnp.concatenate(lines, axis=0).astype(BF16), spread, preferred_element_type=F32
        )
        bias[h] = jnp.where(allowed > 0.5, 0.0, -jnp.inf)

    def duplicates(i, act):
        @pl.when((i == jnp.maximum(SUB * z, SUB)) & (z + 1 < U))
        def _():
            for s in range(half):
                act(d_copy(s, du_s.at[s], z + 1))

        @pl.when((i == jnp.maximum(SUB * (U - 1 - z), SUB)) & (z > 0))
        def _():
            for s in range(half):
                act(d_copy(s, dd_s.at[s], z - 1))

    def streams(i, arrive, act):
        s = lax.rem(i, SUB)
        hops = 1 + i // SUB
        crosses = (hops > 1) | (s >= half)
        for step in (1, -1):
            zz = z - step * hops
            slot = zz * SUB + s

            @pl.when((zz >= 0) & (zz < U))
            def _():
                if arrive:
                    z_copy(slot, zs.at[slot], lax.rem(z + 1, U)).wait_recv()

                @pl.when((z + step >= 0) & (z + step < U))
                def _():
                    act(z_copy(slot, zs.at[slot], z + step))

                @pl.when(crosses)
                def _():
                    act(x_copy(slot))

                act(c_copy(slot))

    log2e = 1.4426950408889634
    factor = log2e / math.sqrt(HD)

    def logits(h, qv, q0, nq, k0, nk):
        keys = kv[0, h, pl.ds(k0, nk)].reshape(nk * BR, HD)
        s = lax.dot_general(qv, keys, (((1,), (1,)), ((), ())), preferred_element_type=F32)
        at = pl.ds(pl.multiple_of(k0 * BR, 128), nk * BR)
        return jnp.concatenate(
            [s[r * R:(r + 1) * R] * factor + bias[h, pl.ds(q0 + r, 1), at] for r in range(nq)], axis=0
        )

    def weigh(h, s, new, k0, nk):
        width = nk * BR
        p = jnp.exp2(s - jnp.concatenate([new] * (width // HD), axis=1))
        total = p[:, :HD]
        for j in range(1, width // HD):
            total = total + p[:, j * HD:(j + 1) * HD]
        values = kv[1, h, pl.ds(k0, nk)].reshape(width, HD)
        return total, jnp.dot(p.astype(BF16), values, preferred_element_type=F32)

    def fresh(h, i, nk):
        at = pl.ds(pl.multiple_of(i * R2, R2), R2)
        s = logits(h, q[h, at, :], 2 * i, 2, 0, nk)
        new = jnp.broadcast_to(jnp.maximum(jnp.max(s, axis=1, keepdims=True), LOW), (R2, HD))
        high[h, at, :] = new
        den[h, at, :], num[h, at, :] = weigh(h, s, new, 0, nk)

    def update(h, at, q0, nq, k0, nk):
        s = logits(h, q[h, at, :], q0, nq, k0, nk)
        old = high[h, at, :]
        new = jnp.maximum(old, jnp.max(s, axis=1, keepdims=True))
        total, product = weigh(h, s, new, k0, nk)
        fix = jnp.exp2(old - new)
        return new, den[h, at, :] * fix + total, num[h, at, :] * fix + product

    def attend(k):
        for h in range(H):
            if k > 0:
                at = pl.ds(0, k * R2)
                high[h, at, :], den[h, at, :], num[h, at, :] = update(h, at, 0, 2 * k, 2 * k, 2)
            fresh(h, k, 2 * (k + 1))

    def kv_wait(i, h):
        for d in range(1, B):
            kv_copy(lax.rem(y + d, B), i, h, d).wait_recv()

    def project(i):
        first, second = pick(slots, 2 * i), pick(slots, 2 * i + 1)
        at = pl.ds(pl.multiple_of(i * R2, R2), R2)
        mine = pl.ds(pl.multiple_of(y * R, R), R)

        def term(c, k):
            return jnp.dot(
                jnp.concatenate([g[first, k], g[second, k]], axis=0),
                w[c, pl.ds(pl.multiple_of(k * feats, feats), feats), :],
                preferred_element_type=F32,
            )

        for slot in (first, second):
            c_arrival(slot).wait_recv()
        for c in range(3):
            sums[c] = term(c, t) + term(c, near) + term(c, far)
        for slot in (first, second):
            f_arrival(slot).wait_recv()
        for c in (1, 2, 0):
            acc = sums[c] + term(c, cross)
            for h in range(H):
                val = (acc[:, h * HD:(h + 1) * HD] * scale_ref[h, c]).astype(BF16)
                if c == 0:
                    q[h, at, :] = val
                else:
                    kv[c - 1, h, 2 * i, mine, :] = val[:R]
                    kv[c - 1, h, 2 * i + 1, mine, :] = val[R:]
                if c == 2:
                    for d in range(1, B):
                        kv_copy(y, i, h, d).start()

    def pair(i, carry):
        for e in range(2):
            n = 2 * i + e
            duplicates(n, lambda c: c.start())
            streams(n, True, lambda c: c.start())
            slot = pick(slots, n)
            x_arrival(slot).wait_recv()
            f_copy(slot).start()

        @pl.when(i == 0)
        def _():
            w_copy.wait()
            for s in range(SUB):
                own_copy(s).wait()

        @pl.when(i == 1)
        def _():
            for c in wo_copies:
                c.start()

        project(i)

        for k in range(NP - 1):
            @pl.when(i == k + 1)
            def _():
                for h in range(H):
                    kv_wait(k, h)
                attend(k)

        return carry

    lax.fori_loop(0, NP, pair, 0)
    for h in range(H):
        fresh(h, NP - 1, 2 * (NP - 1))
    RC = rows // PARTS
    RW = rows // WIDE
    per = PARTS // SUB

    def chunk(c, size=RC):
        return pl.ds(pl.multiple_of(c * size, size), size)

    def at_place(zz, c):
        first = pick(places, zz * SUB + c // per) * R + lax.rem(c, per) * RC
        return pl.ds(pl.multiple_of(first, RC), RC)

    def a_copy(c, h, zz, src):
        return remote(
            att.at[h, at_place(zz, c)],
            arr.at[src, chunk(c), pl.ds(h * HD, HD)],
            as_.at[zz, c, h],
            ar.at[src, c, h],
            ulysses=zz,
        )

    def spread_out(c, h):
        for zz in range(U):
            @pl.when(z != zz)
            def _():
                a_copy(c, h, zz, z).start()

    for h in range(H):
        kv_wait(NP - 1, h)
        _, weight, value = update(h, pl.ds(0, N * R), 0, N, 2 * (NP - 1), 2)
        att[h] = (value / jnp.sum(weight, axis=1, keepdims=True)).astype(BF16)
        if h < H - 1:
            spread_out(0, h)

    def spread_rest(c, carry):
        spread_out(c, H - 1)

        @pl.when(c + 1 < PARTS)
        def _():
            for h in range(H - 1):
                spread_out(c + 1, h)

        for h in range(H):
            arr[z, chunk(c), h * HD:(h + 1) * HD] = att[h, at_place(z, c), :]
        return carry

    lax.fori_loop(0, PARTS, spread_rest, 0)
    for c in wo_copies:
        c.wait()

    def product(at, col):
        acc = jnp.dot(arr[0, at, :], wo[col, 0], preferred_element_type=F32)
        for u in range(1, U):
            acc += jnp.dot(arr[u, at, :], wo[col, u], preferred_element_type=F32)
        return acc

    def p_copy(c):
        return remote(part.at[chunk(c)], got.at[chunk(c)], ps.at[c], pr.at[c], tensor=near)

    def b_copy(c):
        at = chunk(c, RW)
        return remote(back.at[at], back_got.at[at], bs.at[c], br.at[c], tensor=near)

    def m_copy(c):
        return remote(mid.at[chunk(c)], far_out.at[chunk(c)], ms.at[c], mr.at[c], tensor=far)

    def h_copy(c):
        return pltpu.make_async_copy(here.at[chunk(c, RW)], near_out.at[chunk(c, RW)], hs.at[c])

    def lead(c):
        at = chunk(c)
        for d in range(1, U):
            for h in range(H):
                zz = lax.rem(z + d, U)
                a_copy(c, h, zz, zz).wait_recv()
        part[at] = product(at, cross).astype(BF16)
        p_copy(c).start()

    def follow(c):
        at = chunk(c)
        there = product(at, far)
        p_copy(c).wait_recv()
        mid[at] = (there + got[at].astype(F32)).astype(BF16)
        m_copy(c).start()

    def outward(c, carry):
        lead(c + 1)
        follow(c)
        return carry

    lead(0)
    follow(0)
    lead(1)
    lax.fori_loop(1, PARTS - 1, outward, 0)
    follow(PARTS - 1)

    for c in range(WIDE):
        at = chunk(c, RW)
        back[at] = product(at, near).astype(BF16)
        b_copy(c).start()
        here[at] = product(at, t)
    for c in range(WIDE):
        at = chunk(c, RW)
        b_copy(c).wait_recv()
        here[at] = here[at] + back_got[at].astype(F32)
        h_copy(c).start()

    own_sends(lambda c: c.wait_send())

    def drain(i, carry):
        duplicates(i, lambda c: c.wait_send())
        streams(i, False, lambda c: c.wait_send())
        f_copy(i).wait_send()
        return carry

    lax.fori_loop(0, N, drain, 0)

    def kv_drain(i, carry):
        for h in range(H):
            for d in range(1, B):
                kv_copy(y, i, h, d).wait_send()
        return carry

    lax.fori_loop(0, NP, kv_drain, 0)

    def out_drain(c, carry):
        for d in range(1, U):
            for h in range(H):
                a_copy(c, h, lax.rem(z + d, U), z).wait_send()
        p_copy(c).wait_send()
        m_copy(c).wait_send()
        m_copy(c).wait_recv()
        return carry

    lax.fori_loop(0, PARTS, out_drain, 0)
    for c in range(WIDE):
        b_copy(c).wait_send()
        h_copy(c).wait()


def local(tokens, w_qkv, qkv_scale, block_mask, w_out):
    U, B, T = lax.axis_size("ulysses"), lax.axis_size("blk"), lax.axis_size("tensor")
    rows, feats = tokens.shape
    heads = block_mask.shape[0]
    cols = w_qkv.shape[2]
    hd = cols // heads
    R, N = rows // SUB, U * SUB
    dma = lambda *s: pltpu.SemaphoreType.DMA(s)
    near_sum, far_sum = pl.pallas_call(
        functools.partial(kernel, U, B, T),
        out_shape=(pltpu.VMEM((rows, feats), F32), pltpu.VMEM((rows, feats), BF16)),
        in_specs=[pl.BlockSpec(memory_space=pltpu.HBM)] * 5,
        out_specs=(pl.BlockSpec(memory_space=pl.ANY),) * 2,
        scratch_shapes=[
            pltpu.VMEM((N, T, R, feats), BF16),
            pltpu.VMEM((3, T * feats, cols), BF16),
            pltpu.VMEM((T, U, cols, feats), BF16),
            pltpu.VMEM((heads, U * rows, hd), BF16),
            pltpu.VMEM((2, heads, N, B * R, hd), BF16),
            pltpu.VMEM((heads, N, N * B * R), F32),
            pltpu.VMEM((heads, U * rows, hd), F32),
            pltpu.VMEM((heads, U * rows, hd), F32),
            pltpu.VMEM((heads, U * rows, hd), F32),
            pltpu.VMEM((heads, U * rows, hd), BF16),
            pltpu.VMEM((U, rows, cols), BF16),
            pltpu.VMEM((rows, feats), BF16),
            pltpu.VMEM((rows, feats), BF16),
            pltpu.VMEM((rows, feats), BF16),
            pltpu.VMEM((rows, feats), BF16),
            pltpu.VMEM((rows, feats), BF16),
            pltpu.VMEM((rows, feats), F32),
            pltpu.VMEM((3, 2 * R, cols), F32),
            pltpu.SMEM(qkv_scale.T.shape, F32),
            pltpu.VMEM(block_mask.shape, jnp.int32),
            dma(2),
            pltpu.SemaphoreType.DMA,
            dma(T),
            dma(SUB),
            dma(N), dma(N), dma(SUB), dma(SUB), dma(SUB), dma(SUB),
            dma(N), dma(N), dma(N), dma(N), dma(N), dma(N),
            dma(B, N // 2, heads), dma(B, N // 2, heads),
            dma(U, PARTS, heads), dma(U, PARTS, heads),
            dma(PARTS), dma(PARTS), dma(WIDE), dma(WIDE), dma(PARTS), dma(PARTS), dma(WIDE),
        ],
        compiler_params=pltpu.CompilerParams(
            collective_id=0, has_side_effects=True, vmem_limit_bytes=54 * 1024 * 1024
        ),
    )(*(
        pltpu.with_memory_space_constraint(a, pltpu.HBM)
        for a in (tokens, jnp.transpose(w_qkv, (1, 0, 2)), qkv_scale.T, block_mask, w_out)
    ))
    return (near_sum + far_sum.astype(F32)).astype(BF16)


def solution(mesh):
    return jax.shard_map(
        local,
        mesh=mesh,
        in_specs=(
            P(("ulysses", "blk"), "tensor"),
            P(None, None, ("ulysses", "tensor")),
            P(None, ("ulysses", "tensor")),
            P(("ulysses", "tensor"), None, None),
            P(None, "tensor", None),
        ),
        out_specs=P(("ulysses", "blk"), "tensor"),
        check_vma=False,
    )
```

```python
import functools
import math

import jax
import jax.numpy as jnp
from jax import lax
from jax.experimental import pallas as pl
from jax.experimental.pallas import tpu as pltpu
from jax.sharding import PartitionSpec as P

SUB = 4
PARTS = 4
WIDE = 2
F32 = jnp.float32
BF16 = jnp.bfloat16
LOW = -1e30


def by_z(z, zz, s):
    return abs(z - zz) == 1 and s < SUB // 2


def orders(U):
    got = [{(z, s): 0 for s in range(SUB)} for z in range(U)]
    extra = [{} for _ in range(U)]
    for step in (1, -1):
        for a in range(U) if step == 1 else range(U - 1, -1, -1):
            b, free = a + step, 0
            if not 0 <= b < U:
                continue
            zz = a
            while 0 <= zz < U:
                for s in range(SUB):
                    free = max(free, got[a][zz, s]) + 1
                    got[b][zz, s] = free
                zz -= step
            for s in range(SUB // 2):
                free = max(free, s + 1) + 1
                extra[b][a, s] = free
    result = []
    for z in range(U):
        sent = [(z, s) for s in range(SUB)]
        for i in range(SUB * U):
            for zz in (z - 1 - i // SUB, z + 1 + i // SUB):
                if 0 <= zz < U and not by_z(z, zz, i % SUB):
                    sent.append((zz, i % SUB))
        free, done = 0, dict(extra[z])
        for piece in sent:
            free = max(free, got[z][piece]) + 1
            done[piece] = free
        ranked = sorted(done, key=lambda p: (max(done[p], got[z][p]), p))
        result.append([zz * SUB + s for zz, s in ranked])
    return result


def kernel(U, B, T, x_hbm, w_hbm, scale_hbm, mask_hbm, wo_hbm, near_out, far_out,
           g, w, wo, q, kv, bias, high, den, num, att, arr, part, got, back, back_got, mid, here, sums,
           scale_ref, mask_ref, small_sem,
           w_sem, wo_sem, own_sem,
           zs, zr, up_s, dn_s, du_s, dd_s, xs, xr, cs, cr, fs, fr, ks, kr, as_, ar, ps, pr, bs, br, ms, mr, hs):
    z, y, t = lax.axis_index("ulysses"), lax.axis_index("blk"), lax.axis_index("tensor")
    near = t + 1 - 2 * lax.rem(t, 2)
    far = lax.rem(t + T // 2, T)
    cross = lax.rem(near + T // 2, T)
    rows, feats = x_hbm.shape
    R = rows // SUB
    H, HD = q.shape[0], q.shape[2]
    N = U * SUB
    NP = N // 2
    R2 = 2 * R
    BR = B * R
    blocks = mask_ref.shape[1]
    nbp = blocks // (U * B)
    block = rows // nbp
    half = SUB // 2

    barrier = pltpu.get_barrier_semaphore()
    for step in (1, -1):
        @pl.when((z + step >= 0) & (z + step < U))
        def _():
            pl.semaphore_signal(barrier, inc=1, device_id={"ulysses": z + step})
    for d in range(1, B):
        pl.semaphore_signal(barrier, inc=1, device_id={"blk": lax.rem(y + d, B)})
    pl.semaphore_signal(barrier, inc=1, device_id={"tensor": near})
    pl.semaphore_signal(barrier, inc=1, device_id={"tensor": far})

    table = orders(U)
    place = [[order.index(n) for n in range(N)] for order in table]

    def at_z(values):
        out = values[-1]
        for u in range(U - 2, -1, -1):
            out = jnp.where(z == u, values[u], out)
        return out

    slots = [at_z([table[u][n] for u in range(U)]) for n in range(N)]
    places = [at_z([place[u][n] for u in range(U)]) for n in range(N)]

    def pick(values, i):
        out = values[-1]
        for n in range(N - 2, -1, -1):
            out = jnp.where(i == n, values[n], out)
        return out

    def remote(src, dst, send, recv, **where):
        return pltpu.make_async_remote_copy(
            src_ref=src, dst_ref=dst, send_sem=send, recv_sem=recv, device_id=where
        )

    def own_copy(s):
        return pltpu.make_async_copy(x_hbm.at[pl.ds(s * R, R)], g.at[z * SUB + s, t], own_sem.at[s])

    def source(slot, s, own):
        return x_hbm.at[pl.ds(s * R, R)] if own else g.at[slot, t]

    def z_copy(slot, send, target, src=None):
        return remote(g.at[slot, t] if src is None else src, g.at[slot, t], send, zr.at[slot], ulysses=target)

    def x_copy(slot, src=None):
        return remote(g.at[slot, t] if src is None else src, g.at[slot, t], xs.at[slot], xr.at[slot], tensor=far)

    def c_copy(slot, src=None):
        return remote(g.at[slot, t] if src is None else src, g.at[slot, t], cs.at[slot], cr.at[slot], tensor=near)

    def x_arrival(slot):
        return remote(g.at[slot, far], g.at[slot, far], xs.at[slot], xr.at[slot], tensor=far)

    def c_arrival(slot):
        return remote(g.at[slot, near], g.at[slot, near], cs.at[slot], cr.at[slot], tensor=near)

    def f_copy(slot):
        return remote(g.at[slot, far], g.at[slot, far], fs.at[slot], fr.at[slot], tensor=near)

    def f_arrival(slot):
        return remote(g.at[slot, cross], g.at[slot, cross], fs.at[slot], fr.at[slot], tensor=near)

    def d_copy(s, send, target):
        slot = z * SUB + s
        return remote(g.at[slot, far], g.at[slot, far], send, xr.at[slot], ulysses=target)

    def kv_copy(who, i, h, d):
        view = kv.at[:, h, pl.ds(2 * i, 2), pl.ds(pl.multiple_of(who * R, R), R), :]
        return remote(view, view, ks.at[d - 1, i, h], kr.at[who, i, h], blk=lax.rem(y + d, B))

    w_copy = pltpu.make_async_copy(w_hbm, w, w_sem)
    wo_copies = [
        pltpu.make_async_copy(wo_hbm.at[:, :, pl.ds(j * feats, feats)], wo.at[j], wo_sem.at[j])
        for j in range(T)
    ]

    small = [
        pltpu.make_async_copy(scale_hbm, scale_ref, small_sem.at[0]),
        pltpu.make_async_copy(mask_hbm, mask_ref, small_sem.at[1]),
    ]
    for c in small:
        c.start()

    sides = jnp.where(z > 0, 1, 0) + jnp.where(z + 1 < U, 1, 0)
    pl.semaphore_wait(barrier, sides + (B - 1) + 2)

    def own_sends(act):
        for s in range(SUB):
            slot = z * SUB + s
            src = x_hbm.at[pl.ds(s * R, R)]
            act(x_copy(slot, src))

            @pl.when(z + 1 < U)
            def _():
                act(z_copy(slot, up_s.at[s], z + 1, src))

            @pl.when(z > 0)
            def _():
                act(z_copy(slot, dn_s.at[s], z - 1, src))

            act(c_copy(slot, src))

    own_sends(lambda c: c.start())
    for s in range(SUB):
        own_copy(s).start()
    w_copy.start()
    for c in small:
        c.wait()

    lane = lax.broadcasted_iota(jnp.int32, (1, BR), 1) // R
    key_block = jnp.concatenate(
        [(slots[n] // SUB * B + lane) * nbp + lax.rem(slots[n], SUB) * R // block for n in range(N)], axis=1
    )
    spread = (lax.broadcasted_iota(jnp.int32, (blocks, N * BR), 0) == key_block).astype(F32).astype(BF16)
    ids = lax.broadcasted_iota(jnp.int32, (1, blocks), 1)
    for h in range(H):
        lines = []
        for n in range(N):
            qb = (slots[n] // SUB * B + y) * nbp + lax.rem(slots[n], SUB) * R // block
            lines.append(jnp.where((mask_ref[h, pl.ds(qb, 1), :] == 1) | (ids == qb), 1.0, 0.0))
        allowed = jnp.dot(
            jnp.concatenate(lines, axis=0).astype(BF16), spread, preferred_element_type=F32
        )
        bias[h] = jnp.where(allowed > 0.5, 0.0, -jnp.inf)

    def duplicates(i, act):
        @pl.when((i == jnp.maximum(SUB * z, SUB)) & (z + 1 < U))
        def _():
            for s in range(half):
                act(d_copy(s, du_s.at[s], z + 1))

        @pl.when((i == jnp.maximum(SUB * (U - 1 - z), SUB)) & (z > 0))
        def _():
            for s in range(half):
                act(d_copy(s, dd_s.at[s], z - 1))

    def streams(i, arrive, act):
        s = lax.rem(i, SUB)
        hops = 1 + i // SUB
        crosses = (hops > 1) | (s >= half)
        for step in (1, -1):
            zz = z - step * hops
            slot = zz * SUB + s

            @pl.when((zz >= 0) & (zz < U))
            def _():
                if arrive:
                    z_copy(slot, zs.at[slot], lax.rem(z + 1, U)).wait_recv()

                @pl.when((z + step >= 0) & (z + step < U))
                def _():
                    act(z_copy(slot, zs.at[slot], z + step))

                @pl.when(crosses)
                def _():
                    act(x_copy(slot))

                act(c_copy(slot))

    log2e = 1.4426950408889634
    factor = log2e / math.sqrt(HD)

    def logits(h, qv, q0, nq, k0, nk):
        keys = kv[0, h, pl.ds(k0, nk)].reshape(nk * BR, HD)
        s = lax.dot_general(qv, keys, (((1,), (1,)), ((), ())), preferred_element_type=F32)
        at = pl.ds(pl.multiple_of(k0 * BR, 128), nk * BR)
        return jnp.concatenate(
            [s[r * R:(r + 1) * R] * factor + bias[h, pl.ds(q0 + r, 1), at] for r in range(nq)], axis=0
        )

    def weigh(h, s, new, k0, nk):
        width = nk * BR
        p = jnp.exp2(s - jnp.concatenate([new] * (width // HD), axis=1))
        total = p[:, :HD]
        for j in range(1, width // HD):
            total = total + p[:, j * HD:(j + 1) * HD]
        values = kv[1, h, pl.ds(k0, nk)].reshape(width, HD)
        return total, jnp.dot(p.astype(BF16), values, preferred_element_type=F32)

    def fresh(h, i, nk):
        at = pl.ds(pl.multiple_of(i * R2, R2), R2)
        s = logits(h, q[h, at, :], 2 * i, 2, 0, nk)
        new = jnp.broadcast_to(jnp.maximum(jnp.max(s, axis=1, keepdims=True), LOW), (R2, HD))
        high[h, at, :] = new
        den[h, at, :], num[h, at, :] = weigh(h, s, new, 0, nk)

    def update(h, at, q0, nq, k0, nk):
        s = logits(h, q[h, at, :], q0, nq, k0, nk)
        old = high[h, at, :]
        new = jnp.maximum(old, jnp.max(s, axis=1, keepdims=True))
        total, product = weigh(h, s, new, k0, nk)
        fix = jnp.exp2(old - new)
        return new, den[h, at, :] * fix + total, num[h, at, :] * fix + product

    def attend(k):
        for h in range(H):
            if k > 0:
                at = pl.ds(0, k * R2)
                high[h, at, :], den[h, at, :], num[h, at, :] = update(h, at, 0, 2 * k, 2 * k, 2)
            fresh(h, k, 2 * (k + 1))

    def kv_wait(i, h):
        for d in range(1, B):
            kv_copy(lax.rem(y + d, B), i, h, d).wait_recv()

    def project(i):
        first, second = pick(slots, 2 * i), pick(slots, 2 * i + 1)
        at = pl.ds(pl.multiple_of(i * R2, R2), R2)
        mine = pl.ds(pl.multiple_of(y * R, R), R)

        def term(c, k):
            return jnp.dot(
                jnp.concatenate([g[first, k], g[second, k]], axis=0),
                w[c, pl.ds(pl.multiple_of(k * feats, feats), feats), :],
                preferred_element_type=F32,
            )

        for slot in (first, second):
            c_arrival(slot).wait_recv()
        for c in range(3):
            sums[c] = term(c, t) + term(c, near) + term(c, far)
        for slot in (first, second):
            f_arrival(slot).wait_recv()
        for c in (1, 2, 0):
            acc = sums[c] + term(c, cross)
            for h in range(H):
                val = (acc[:, h * HD:(h + 1) * HD] * scale_ref[h, c]).astype(BF16)
                if c == 0:
                    q[h, at, :] = val
                else:
                    kv[c - 1, h, 2 * i, mine, :] = val[:R]
                    kv[c - 1, h, 2 * i + 1, mine, :] = val[R:]
                if c == 2:
                    for d in range(1, B):
                        kv_copy(y, i, h, d).start()

    def pair(i, carry):
        for e in range(2):
            n = 2 * i + e
            duplicates(n, lambda c: c.start())
            streams(n, True, lambda c: c.start())
            slot = pick(slots, n)
            x_arrival(slot).wait_recv()
            f_copy(slot).start()

        @pl.when(i == 0)
        def _():
            w_copy.wait()
            for s in range(SUB):
                own_copy(s).wait()

        @pl.when(i == 1)
        def _():
            for c in wo_copies:
                c.start()

        project(i)

        for k in range(NP - 1):
            @pl.when(i == k + 1)
            def _():
                for h in range(H):
                    kv_wait(k, h)
                attend(k)

        return carry

    lax.fori_loop(0, NP, pair, 0)
    for h in range(H):
        fresh(h, NP - 1, 2 * (NP - 1))
    RC = rows // PARTS
    RW = rows // WIDE
    per = PARTS // SUB

    def chunk(c, size=RC):
        return pl.ds(pl.multiple_of(c * size, size), size)

    def at_place(zz, c):
        first = pick(places, zz * SUB + c // per) * R + lax.rem(c, per) * RC
        return pl.ds(pl.multiple_of(first, RC), RC)

    def a_copy(c, h, zz, src):
        return remote(
            att.at[h, at_place(zz, c)],
            arr.at[src, chunk(c), pl.ds(h * HD, HD)],
            as_.at[zz, c, h],
            ar.at[src, c, h],
            ulysses=zz,
        )

    def spread_out(c, h):
        for zz in range(U):
            @pl.when(z != zz)
            def _():
                a_copy(c, h, zz, z).start()

    for h in range(H):
        kv_wait(NP - 1, h)
        _, weight, value = update(h, pl.ds(0, N * R), 0, N, 2 * (NP - 1), 2)
        att[h] = (value / jnp.sum(weight, axis=1, keepdims=True)).astype(BF16)
        if h < H - 1:
            spread_out(0, h)

    def spread_rest(c, carry):
        spread_out(c, H - 1)

        @pl.when(c + 1 < PARTS)
        def _():
            for h in range(H - 1):
                spread_out(c + 1, h)

        for h in range(H):
            arr[z, chunk(c), h * HD:(h + 1) * HD] = att[h, at_place(z, c), :]
        return carry

    lax.fori_loop(0, PARTS, spread_rest, 0)
    for c in wo_copies:
        c.wait()

    def product(at, col):
        acc = jnp.dot(arr[0, at, :], wo[col, 0], preferred_element_type=F32)
        for u in range(1, U):
            acc += jnp.dot(arr[u, at, :], wo[col, u], preferred_element_type=F32)
        return acc

    def p_copy(c):
        return remote(part.at[chunk(c)], got.at[chunk(c)], ps.at[c], pr.at[c], tensor=near)

    def b_copy(c):
        at = chunk(c, RW)
        return remote(back.at[at], back_got.at[at], bs.at[c], br.at[c], tensor=near)

    def m_copy(c):
        return remote(mid.at[chunk(c)], far_out.at[chunk(c)], ms.at[c], mr.at[c], tensor=far)

    def h_copy(c):
        return pltpu.make_async_copy(here.at[chunk(c, RW)], near_out.at[chunk(c, RW)], hs.at[c])

    def lead(c):
        at = chunk(c)
        for d in range(1, U):
            for h in range(H):
                zz = lax.rem(z + d, U)
                a_copy(c, h, zz, zz).wait_recv()
        part[at] = product(at, cross).astype(BF16)
        p_copy(c).start()

    def follow(c):
        at = chunk(c)
        there = product(at, far)
        p_copy(c).wait_recv()
        mid[at] = (there + got[at].astype(F32)).astype(BF16)
        m_copy(c).start()

    def outward(c, carry):
        lead(c + 1)
        follow(c)
        return carry

    lead(0)
    follow(0)
    lead(1)
    lax.fori_loop(1, PARTS - 1, outward, 0)
    follow(PARTS - 1)

    for c in range(WIDE):
        at = chunk(c, RW)
        back[at] = product(at, near).astype(BF16)
        b_copy(c).start()
        here[at] = product(at, t)
    for c in range(WIDE):
        at = chunk(c, RW)
        b_copy(c).wait_recv()
        here[at] = here[at] + back_got[at].astype(F32)
        h_copy(c).start()

    own_sends(lambda c: c.wait_send())

    def drain(i, carry):
        duplicates(i, lambda c: c.wait_send())
        streams(i, False, lambda c: c.wait_send())
        f_copy(i).wait_send()
        return carry

    lax.fori_loop(0, N, drain, 0)

    def kv_drain(i, carry):
        for h in range(H):
            for d in range(1, B):
                kv_copy(y, i, h, d).wait_send()
        return carry

    lax.fori_loop(0, NP, kv_drain, 0)

    def out_drain(c, carry):
        for d in range(1, U):
            for h in range(H):
                a_copy(c, h, lax.rem(z + d, U), z).wait_send()
        p_copy(c).wait_send()
        m_copy(c).wait_send()
        m_copy(c).wait_recv()
        return carry

    lax.fori_loop(0, PARTS, out_drain, 0)
    for c in range(WIDE):
        b_copy(c).wait_send()
        h_copy(c).wait()


def local(tokens, w_qkv, qkv_scale, block_mask, w_out):
    U, B, T = lax.axis_size("ulysses"), lax.axis_size("blk"), lax.axis_size("tensor")
    rows, feats = tokens.shape
    heads = block_mask.shape[0]
    cols = w_qkv.shape[2]
    hd = cols // heads
    R, N = rows // SUB, U * SUB
    dma = lambda *s: pltpu.SemaphoreType.DMA(s)
    near_sum, far_sum = pl.pallas_call(
        functools.partial(kernel, U, B, T),
        out_shape=(pltpu.VMEM((rows, feats), F32), pltpu.VMEM((rows, feats), BF16)),
        in_specs=[pl.BlockSpec(memory_space=pltpu.HBM)] * 5,
        out_specs=(pl.BlockSpec(memory_space=pl.ANY),) * 2,
        scratch_shapes=[
            pltpu.VMEM((N, T, R, feats), BF16),
            pltpu.VMEM((3, T * feats, cols), BF16),
            pltpu.VMEM((T, U, cols, feats), BF16),
            pltpu.VMEM((heads, U * rows, hd), BF16),
            pltpu.VMEM((2, heads, N, B * R, hd), BF16),
            pltpu.VMEM((heads, N, N * B * R), F32),
            pltpu.VMEM((heads, U * rows, hd), F32),
            pltpu.VMEM((heads, U * rows, hd), F32),
            pltpu.VMEM((heads, U * rows, hd), F32),
            pltpu.VMEM((heads, U * rows, hd), BF16),
            pltpu.VMEM((U, rows, cols), BF16),
            pltpu.VMEM((rows, feats), BF16),
            pltpu.VMEM((rows, feats), BF16),
            pltpu.VMEM((rows, feats), BF16),
            pltpu.VMEM((rows, feats), BF16),
            pltpu.VMEM((rows, feats), BF16),
            pltpu.VMEM((rows, feats), F32),
            pltpu.VMEM((3, 2 * R, cols), F32),
            pltpu.SMEM(qkv_scale.T.shape, F32),
            pltpu.VMEM(block_mask.shape, jnp.int32),
            dma(2),
            pltpu.SemaphoreType.DMA,
            dma(T),
            dma(SUB),
            dma(N), dma(N), dma(SUB), dma(SUB), dma(SUB), dma(SUB),
            dma(N), dma(N), dma(N), dma(N), dma(N), dma(N),
            dma(B, N // 2, heads), dma(B, N // 2, heads),
            dma(U, PARTS, heads), dma(U, PARTS, heads),
            dma(PARTS), dma(PARTS), dma(WIDE), dma(WIDE), dma(PARTS), dma(PARTS), dma(WIDE),
        ],
        compiler_params=pltpu.CompilerParams(
            collective_id=0, has_side_effects=True, vmem_limit_bytes=54 * 1024 * 1024
        ),
    )(*(
        pltpu.with_memory_space_constraint(a, pltpu.HBM)
        for a in (tokens, jnp.transpose(w_qkv, (1, 0, 2)), qkv_scale.T, block_mask, w_out)
    ))
    return (near_sum + far_sum.astype(F32)).astype(BF16)


def solution(mesh):
    return jax.shard_map(
        local,
        mesh=mesh,
        in_specs=(
            P(("ulysses", "blk"), "tensor"),
            P(None, None, ("ulysses", "tensor")),
            P(None, ("ulysses", "tensor")),
            P(("ulysses", "tensor"), None, None),
            P(None, "tensor", None),
        ),
        out_specs=P(("ulysses", "blk"), "tensor"),
        check_vma=False,
    )
```

```python
import functools
import math

import jax
import jax.numpy as jnp
from jax import lax
from jax.experimental import pallas as pl
from jax.experimental.pallas import tpu as pltpu
from jax.sharding import PartitionSpec as P

SUB = 4
PARTS = 4
WIDE = 2
F32 = jnp.float32
BF16 = jnp.bfloat16
LOW = -1e30


def by_z(z, zz, s):
    return abs(z - zz) == 1 and s < SUB // 2


def orders(U):
    got = [{(z, s): 0 for s in range(SUB)} for z in range(U)]
    extra = [{} for _ in range(U)]
    for step in (1, -1):
        for a in range(U) if step == 1 else range(U - 1, -1, -1):
            b, free = a + step, 0
            if not 0 <= b < U:
                continue
            zz = a
            while 0 <= zz < U:
                for s in range(SUB):
                    free = max(free, got[a][zz, s]) + 1
                    got[b][zz, s] = free
                zz -= step
            for s in range(SUB // 2):
                free = max(free, s + 1) + 1
                extra[b][a, s] = free
    result = []
    for z in range(U):
        sent = [(z, s) for s in range(SUB)]
        for i in range(SUB * U):
            for zz in (z - 1 - i // SUB, z + 1 + i // SUB):
                if 0 <= zz < U and not by_z(z, zz, i % SUB):
                    sent.append((zz, i % SUB))
        free, done = 0, dict(extra[z])
        for piece in sent:
            free = max(free, got[z][piece]) + 1
            done[piece] = free
        ranked = sorted(done, key=lambda p: (max(done[p], got[z][p]), p))
        result.append([zz * SUB + s for zz, s in ranked])
    return result


def kernel(U, B, T, x_hbm, w_hbm, scale_hbm, mask_hbm, wo_hbm, near_out, far_out,
           g, w, wo, q, kv, bias, high, den, num, att, arr, part, got, back, back_got, mid, here, sums,
           scale_ref, mask_ref, small_sem,
           w_sem, wo_sem, own_sem,
           zs, zr, up_s, dn_s, du_s, dd_s, xs, xr, cs, cr, fs, fr, ks, kr, as_, ar, ps, pr, bs, br, ms, mr, hs):
    z, y, t = lax.axis_index("ulysses"), lax.axis_index("blk"), lax.axis_index("tensor")
    near = t + 1 - 2 * lax.rem(t, 2)
    far = lax.rem(t + T // 2, T)
    cross = lax.rem(near + T // 2, T)
    rows, feats = x_hbm.shape
    R = rows // SUB
    H, HD = q.shape[0], q.shape[2]
    N = U * SUB
    NP = N // 2
    R2 = 2 * R
    BR = B * R
    blocks = mask_ref.shape[1]
    nbp = blocks // (U * B)
    block = rows // nbp
    half = SUB // 2

    barrier = pltpu.get_barrier_semaphore()
    for step in (1, -1):
        @pl.when((z + step >= 0) & (z + step < U))
        def _():
            pl.semaphore_signal(barrier, inc=1, device_id={"ulysses": z + step})
    for d in range(1, B):
        pl.semaphore_signal(barrier, inc=1, device_id={"blk": lax.rem(y + d, B)})
    pl.semaphore_signal(barrier, inc=1, device_id={"tensor": near})
    pl.semaphore_signal(barrier, inc=1, device_id={"tensor": far})

    table = orders(U)
    place = [[order.index(n) for n in range(N)] for order in table]

    def at_z(values):
        out = values[-1]
        for u in range(U - 2, -1, -1):
            out = jnp.where(z == u, values[u], out)
        return out

    slots = [at_z([table[u][n] for u in range(U)]) for n in range(N)]
    places = [at_z([place[u][n] for u in range(U)]) for n in range(N)]

    def pick(values, i):
        out = values[-1]
        for n in range(N - 2, -1, -1):
            out = jnp.where(i == n, values[n], out)
        return out

    def remote(src, dst, send, recv, **where):
        return pltpu.make_async_remote_copy(
            src_ref=src, dst_ref=dst, send_sem=send, recv_sem=recv, device_id=where
        )

    def own_copy(s):
        return pltpu.make_async_copy(x_hbm.at[pl.ds(s * R, R)], g.at[z * SUB + s, t], own_sem.at[s])

    def source(slot, s, own):
        return x_hbm.at[pl.ds(s * R, R)] if own else g.at[slot, t]

    def z_copy(slot, send, target, src=None):
        return remote(g.at[slot, t] if src is None else src, g.at[slot, t], send, zr.at[slot], ulysses=target)

    def x_copy(slot, src=None):
        return remote(g.at[slot, t] if src is None else src, g.at[slot, t], xs.at[slot], xr.at[slot], tensor=far)

    def c_copy(slot, src=None):
        return remote(g.at[slot, t] if src is None else src, g.at[slot, t], cs.at[slot], cr.at[slot], tensor=near)

    def x_arrival(slot):
        return remote(g.at[slot, far], g.at[slot, far], xs.at[slot], xr.at[slot], tensor=far)

    def c_arrival(slot):
        return remote(g.at[slot, near], g.at[slot, near], cs.at[slot], cr.at[slot], tensor=near)

    def f_copy(slot):
        return remote(g.at[slot, far], g.at[slot, far], fs.at[slot], fr.at[slot], tensor=near)

    def f_arrival(slot):
        return remote(g.at[slot, cross], g.at[slot, cross], fs.at[slot], fr.at[slot], tensor=near)

    def d_copy(s, send, target):
        slot = z * SUB + s
        return remote(g.at[slot, far], g.at[slot, far], send, xr.at[slot], ulysses=target)

    def kv_copy(who, i, h, d):
        view = kv.at[:, h, pl.ds(2 * i, 2), pl.ds(pl.multiple_of(who * R, R), R), :]
        return remote(view, view, ks.at[d - 1, i, h], kr.at[who, i, h], blk=lax.rem(y + d, B))

    w_copy = pltpu.make_async_copy(w_hbm, w, w_sem)
    wo_copies = [
        pltpu.make_async_copy(wo_hbm.at[:, :, pl.ds(j * feats, feats)], wo.at[j], wo_sem.at[j])
        for j in range(T)
    ]

    small = [
        pltpu.make_async_copy(scale_hbm, scale_ref, small_sem.at[0]),
        pltpu.make_async_copy(mask_hbm, mask_ref, small_sem.at[1]),
    ]
    for c in small:
        c.start()

    sides = jnp.where(z > 0, 1, 0) + jnp.where(z + 1 < U, 1, 0)
    pl.semaphore_wait(barrier, sides + (B - 1) + 2)

    def own_sends(act):
        for s in range(SUB):
            slot = z * SUB + s
            src = x_hbm.at[pl.ds(s * R, R)]
            act(x_copy(slot, src))

            @pl.when(z + 1 < U)
            def _():
                act(z_copy(slot, up_s.at[s], z + 1, src))

            @pl.when(z > 0)
            def _():
                act(z_copy(slot, dn_s.at[s], z - 1, src))

            act(c_copy(slot, src))

    own_sends(lambda c: c.start())
    for s in range(SUB):
        own_copy(s).start()
    w_copy.start()
    for c in small:
        c.wait()

    lane = lax.broadcasted_iota(jnp.int32, (1, BR), 1) // R
    key_block = jnp.concatenate(
        [(slots[n] // SUB * B + lane) * nbp + lax.rem(slots[n], SUB) * R // block for n in range(N)], axis=1
    )
    spread = (lax.broadcasted_iota(jnp.int32, (blocks, N * BR), 0) == key_block).astype(F32).astype(BF16)
    ids = lax.broadcasted_iota(jnp.int32, (1, blocks), 1)
    for h in range(H):
        lines = []
        for n in range(N):
            qb = (slots[n] // SUB * B + y) * nbp + lax.rem(slots[n], SUB) * R // block
            lines.append(jnp.where((mask_ref[h, pl.ds(qb, 1), :] == 1) | (ids == qb), 1.0, 0.0))
        allowed = jnp.dot(
            jnp.concatenate(lines, axis=0).astype(BF16), spread, preferred_element_type=F32
        )
        bias[h] = jnp.where(allowed > 0.5, 0.0, -jnp.inf)

    def duplicates(i, act):
        @pl.when((i == jnp.maximum(SUB * z, SUB)) & (z + 1 < U))
        def _():
            for s in range(half):
                act(d_copy(s, du_s.at[s], z + 1))

        @pl.when((i == jnp.maximum(SUB * (U - 1 - z), SUB)) & (z > 0))
        def _():
            for s in range(half):
                act(d_copy(s, dd_s.at[s], z - 1))

    def streams(i, arrive, act):
        s = lax.rem(i, SUB)
        hops = 1 + i // SUB
        crosses = (hops > 1) | (s >= half)
        for step in (1, -1):
            zz = z - step * hops
            slot = zz * SUB + s

            @pl.when((zz >= 0) & (zz < U))
            def _():
                if arrive:
                    z_copy(slot, zs.at[slot], lax.rem(z + 1, U)).wait_recv()

                @pl.when((z + step >= 0) & (z + step < U))
                def _():
                    act(z_copy(slot, zs.at[slot], z + step))

                @pl.when(crosses)
                def _():
                    act(x_copy(slot))

                act(c_copy(slot))

    log2e = 1.4426950408889634
    factor = log2e / math.sqrt(HD)

    def logits(h, qv, q0, nq, k0, nk):
        keys = kv[0, h, pl.ds(k0, nk)].reshape(nk * BR, HD)
        s = lax.dot_general(qv, keys, (((1,), (1,)), ((), ())), preferred_element_type=F32)
        at = pl.ds(pl.multiple_of(k0 * BR, 128), nk * BR)
        return jnp.concatenate(
            [s[r * R:(r + 1) * R] * factor + bias[h, pl.ds(q0 + r, 1), at] for r in range(nq)], axis=0
        )

    def weigh(h, s, new, k0, nk):
        width = nk * BR
        p = jnp.exp2(s - jnp.concatenate([new] * (width // HD), axis=1))
        total = p[:, :HD]
        for j in range(1, width // HD):
            total = total + p[:, j * HD:(j + 1) * HD]
        values = kv[1, h, pl.ds(k0, nk)].reshape(width, HD)
        return total, jnp.dot(p.astype(BF16), values, preferred_element_type=F32)

    def fresh(h, i, nk):
        at = pl.ds(pl.multiple_of(i * R2, R2), R2)
        s = logits(h, q[h, at, :], 2 * i, 2, 0, nk)
        new = jnp.broadcast_to(jnp.maximum(jnp.max(s, axis=1, keepdims=True), LOW), (R2, HD))
        high[h, at, :] = new
        den[h, at, :], num[h, at, :] = weigh(h, s, new, 0, nk)

    def update(h, at, q0, nq, k0, nk):
        s = logits(h, q[h, at, :], q0, nq, k0, nk)
        old = high[h, at, :]
        new = jnp.maximum(old, jnp.max(s, axis=1, keepdims=True))
        total, product = weigh(h, s, new, k0, nk)
        fix = jnp.exp2(old - new)
        return new, den[h, at, :] * fix + total, num[h, at, :] * fix + product

    def attend(k):
        for h in range(H):
            if k > 0:
                at = pl.ds(0, k * R2)
                high[h, at, :], den[h, at, :], num[h, at, :] = update(h, at, 0, 2 * k, 2 * k, 2)
            fresh(h, k, 2 * (k + 1))

    def kv_wait(i, h):
        for d in range(1, B):
            kv_copy(lax.rem(y + d, B), i, h, d).wait_recv()

    def project(i):
        first, second = pick(slots, 2 * i), pick(slots, 2 * i + 1)
        at = pl.ds(pl.multiple_of(i * R2, R2), R2)
        mine = pl.ds(pl.multiple_of(y * R, R), R)

        def term(c, k):
            return jnp.dot(
                jnp.concatenate([g[first, k], g[second, k]], axis=0),
                w[c, pl.ds(pl.multiple_of(k * feats, feats), feats), :],
                preferred_element_type=F32,
            )

        for slot in (first, second):
            c_arrival(slot).wait_recv()
        for c in range(3):
            sums[c] = term(c, t) + term(c, near) + term(c, far)
        for slot in (first, second):
            f_arrival(slot).wait_recv()
        for c in (1, 2, 0):
            acc = sums[c] + term(c, cross)
            for h in range(H):
                val = (acc[:, h * HD:(h + 1) * HD] * scale_ref[h, c]).astype(BF16)
                if c == 0:
                    q[h, at, :] = val
                else:
                    kv[c - 1, h, 2 * i, mine, :] = val[:R]
                    kv[c - 1, h, 2 * i + 1, mine, :] = val[R:]
                if c == 2:
                    for d in range(1, B):
                        kv_copy(y, i, h, d).start()

    def pair(i, carry):
        for e in range(2):
            n = 2 * i + e
            duplicates(n, lambda c: c.start())
            streams(n, True, lambda c: c.start())
            slot = pick(slots, n)
            x_arrival(slot).wait_recv()
            f_copy(slot).start()

        @pl.when(i == 0)
        def _():
            w_copy.wait()
            for s in range(SUB):
                own_copy(s).wait()

        @pl.when(i == 1)
        def _():
            for c in wo_copies:
                c.start()

        project(i)

        for k in range(NP - 1):
            @pl.when(i == k + 1)
            def _():
                for h in range(H):
                    kv_wait(k, h)
                attend(k)

        return carry

    lax.fori_loop(0, NP, pair, 0)
    for h in range(H):
        fresh(h, NP - 1, 2 * (NP - 1))
    RC = rows // PARTS
    RW = rows // WIDE
    per = PARTS // SUB

    def chunk(c, size=RC):
        return pl.ds(pl.multiple_of(c * size, size), size)

    def at_place(zz, c):
        first = pick(places, zz * SUB + c // per) * R + lax.rem(c, per) * RC
        return pl.ds(pl.multiple_of(first, RC), RC)

    def a_copy(c, h, zz, src):
        return remote(
            att.at[h, at_place(zz, c)],
            arr.at[src, chunk(c), pl.ds(h * HD, HD)],
            as_.at[zz, c, h],
            ar.at[src, c, h],
            ulysses=zz,
        )

    def spread_out(c, h):
        for d in range(U - 1, 0, -1):
            for zz in (z - d, z + d):
                @pl.when((zz >= 0) & (zz < U))
                def _():
                    a_copy(c, h, zz, z).start()

    for h in range(H):
        kv_wait(NP - 1, h)
        _, weight, value = update(h, pl.ds(0, N * R), 0, N, 2 * (NP - 1), 2)
        att[h] = (value / jnp.sum(weight, axis=1, keepdims=True)).astype(BF16)
        if h < H - 1:
            spread_out(0, h)

    def spread_rest(c, carry):
        spread_out(c, H - 1)

        @pl.when(c + 1 < PARTS)
        def _():
            for h in range(H - 1):
                spread_out(c + 1, h)

        for h in range(H):
            arr[z, chunk(c), h * HD:(h + 1) * HD] = att[h, at_place(z, c), :]
        return carry

    lax.fori_loop(0, PARTS, spread_rest, 0)
    for c in wo_copies:
        c.wait()

    def product(at, col):
        acc = jnp.dot(arr[0, at, :], wo[col, 0], preferred_element_type=F32)
        for u in range(1, U):
            acc += jnp.dot(arr[u, at, :], wo[col, u], preferred_element_type=F32)
        return acc

    def p_copy(c):
        return remote(part.at[chunk(c)], got.at[chunk(c)], ps.at[c], pr.at[c], tensor=near)

    def b_copy(c):
        at = chunk(c, RW)
        return remote(back.at[at], back_got.at[at], bs.at[c], br.at[c], tensor=near)

    def m_copy(c):
        return remote(mid.at[chunk(c)], far_out.at[chunk(c)], ms.at[c], mr.at[c], tensor=far)

    def h_copy(c):
        return pltpu.make_async_copy(here.at[chunk(c, RW)], near_out.at[chunk(c, RW)], hs.at[c])

    def outward(c, carry):
        at = chunk(c)

        def term(u, col):
            return jnp.dot(arr[u, at, :], wo[col, u], preferred_element_type=F32)

        here[at] = term(z, far)
        away = term(z, cross)
        for d in range(1, U):
            u = lax.rem(z + d, U)
            for h in range(H):
                a_copy(c, h, u, u).wait_recv()
            away += term(u, cross)
            if d == U - 1:
                part[at] = away.astype(BF16)
                p_copy(c).start()
            here[at] += term(u, far)
        p_copy(c).wait_recv()
        mid[at] = (here[at] + got[at].astype(F32)).astype(BF16)
        m_copy(c).start()
        return carry

    lax.fori_loop(0, PARTS, outward, 0)

    for c in range(WIDE):
        at = chunk(c, RW)
        back[at] = product(at, near).astype(BF16)
        b_copy(c).start()
        here[at] = product(at, t)
    for c in range(WIDE):
        at = chunk(c, RW)
        b_copy(c).wait_recv()
        here[at] = here[at] + back_got[at].astype(F32)
        h_copy(c).start()

    own_sends(lambda c: c.wait_send())

    def drain(i, carry):
        duplicates(i, lambda c: c.wait_send())
        streams(i, False, lambda c: c.wait_send())
        f_copy(i).wait_send()
        return carry

    lax.fori_loop(0, N, drain, 0)

    def kv_drain(i, carry):
        for h in range(H):
            for d in range(1, B):
                kv_copy(y, i, h, d).wait_send()
        return carry

    lax.fori_loop(0, NP, kv_drain, 0)

    def out_drain(c, carry):
        for d in range(1, U):
            for h in range(H):
                a_copy(c, h, lax.rem(z + d, U), z).wait_send()
        p_copy(c).wait_send()
        m_copy(c).wait_send()
        m_copy(c).wait_recv()
        return carry

    lax.fori_loop(0, PARTS, out_drain, 0)
    for c in range(WIDE):
        b_copy(c).wait_send()
        h_copy(c).wait()


def local(tokens, w_qkv, qkv_scale, block_mask, w_out):
    U, B, T = lax.axis_size("ulysses"), lax.axis_size("blk"), lax.axis_size("tensor")
    rows, feats = tokens.shape
    heads = block_mask.shape[0]
    cols = w_qkv.shape[2]
    hd = cols // heads
    R, N = rows // SUB, U * SUB
    dma = lambda *s: pltpu.SemaphoreType.DMA(s)
    near_sum, far_sum = pl.pallas_call(
        functools.partial(kernel, U, B, T),
        out_shape=(pltpu.VMEM((rows, feats), F32), pltpu.VMEM((rows, feats), BF16)),
        in_specs=[pl.BlockSpec(memory_space=pltpu.HBM)] * 5,
        out_specs=(pl.BlockSpec(memory_space=pl.ANY),) * 2,
        scratch_shapes=[
            pltpu.VMEM((N, T, R, feats), BF16),
            pltpu.VMEM((3, T * feats, cols), BF16),
            pltpu.VMEM((T, U, cols, feats), BF16),
            pltpu.VMEM((heads, U * rows, hd), BF16),
            pltpu.VMEM((2, heads, N, B * R, hd), BF16),
            pltpu.VMEM((heads, N, N * B * R), F32),
            pltpu.VMEM((heads, U * rows, hd), F32),
            pltpu.VMEM((heads, U * rows, hd), F32),
            pltpu.VMEM((heads, U * rows, hd), F32),
            pltpu.VMEM((heads, U * rows, hd), BF16),
            pltpu.VMEM((U, rows, cols), BF16),
            pltpu.VMEM((rows, feats), BF16),
            pltpu.VMEM((rows, feats), BF16),
            pltpu.VMEM((rows, feats), BF16),
            pltpu.VMEM((rows, feats), BF16),
            pltpu.VMEM((rows, feats), BF16),
            pltpu.VMEM((rows, feats), F32),
            pltpu.VMEM((3, 2 * R, cols), F32),
            pltpu.SMEM(qkv_scale.T.shape, F32),
            pltpu.VMEM(block_mask.shape, jnp.int32),
            dma(2),
            pltpu.SemaphoreType.DMA,
            dma(T),
            dma(SUB),
            dma(N), dma(N), dma(SUB), dma(SUB), dma(SUB), dma(SUB),
            dma(N), dma(N), dma(N), dma(N), dma(N), dma(N),
            dma(B, N // 2, heads), dma(B, N // 2, heads),
            dma(U, PARTS, heads), dma(U, PARTS, heads),
            dma(PARTS), dma(PARTS), dma(WIDE), dma(WIDE), dma(PARTS), dma(PARTS), dma(WIDE),
        ],
        compiler_params=pltpu.CompilerParams(
            collective_id=0, has_side_effects=True, vmem_limit_bytes=54 * 1024 * 1024
        ),
    )(*(
        pltpu.with_memory_space_constraint(a, pltpu.HBM)
        for a in (tokens, jnp.transpose(w_qkv, (1, 0, 2)), qkv_scale.T, block_mask, w_out)
    ))
    return (near_sum + far_sum.astype(F32)).astype(BF16)


def solution(mesh):
    return jax.shard_map(
        local,
        mesh=mesh,
        in_specs=(
            P(("ulysses", "blk"), "tensor"),
            P(None, None, ("ulysses", "tensor")),
            P(None, ("ulysses", "tensor")),
            P(("ulysses", "tensor"), None, None),
            P(None, "tensor", None),
        ),
        out_specs=P(("ulysses", "blk"), "tensor"),
        check_vma=False,
    )
```
